32 devices in a mesh: grp: 2 (over x), scan: 16 (over z, y, core).
Axes of the slice: x: 2, y: 2, z: 4, core: 2. Of those that a mesh axis runs over, the one named last changes fastest.
Arguments:
- patterns: bfloat16 [3072, 64, 256], P(('grp', 'scan')), parts along dimension 0, may hold values from -6 to 6
- templates: bfloat16 [32, 64, 256], P('scan'), may hold values from -6 to 6
- radius_bin: int32 [64], replicated, may hold values from 0 to 7
- radial_gain: float32 [8], replicated, may hold values from 0.25 to 4
- orientation: int32 [32, 1], replicated, may hold values from 0 to 15
Outputs:
- corr_map: float32 [3072, 32], P(('grp', 'scan')), parts along dimension 0
- orient_map: float32 [3072, 16], P(('grp', 'scan')), parts along dimension 0
The draws below stay inside these ranges and needn't reach their ends.
There are 2 independent parts, one for each index of `grp`. The reference program is written for one: setup_inputs(seed, part) draws one part's arguments, and reference() takes and returns one part's arrays. A program takes and returns all parts, laid end to end along the dimension named above; an argument that names none is the same for every part. Nothing has to cross between parts.
Inputs may be any that keep to these rules, and one draw needn't show every extreme that they name: Every orientation group holds at least one template.
All inputs are finite; a program needn't handle non-finite values.
Results may differ from the reference program's by a relative error of at most 0.0024.
Values may be sent and summed in bfloat16 or wider, within the bound.
No kernel may reach another device: no remote copies, remote signals or barrier semaphores. Data moves between devices by JAX's collectives and lax.ppermute only.
A program may use at most 128 MiB of HBM per device.

```python
import math
import jax
import jax.numpy as jnp
from jax import lax

RADII = 64
ANGLES = 256
GAINS = 8
POS_DEV = 96
POSITIONS = 1536
TEMPLATES = 32
ORIENTS = 16
N_SCAN = 16


def touch_ends(drawn, stream_key, low, largest):
    longest = drawn.shape.index(max(drawn.shape))
    spots = []
    for shift in (0, 1):
        where = [jax.random.randint(jax.random.fold_in(stream_key, axis), (), 0, length) for axis, length in enumerate(drawn.shape)]
        where[longest] = (where[longest] + shift) % drawn.shape[longest]
        spots.append(tuple(where))
    return drawn.at[spots[0]].set(low).at[spots[1]].set(largest)


def block_levels(stream_key, dims, cuts, low, high):
    factor_of = 1.0
    for axis_at, shards_of in cuts:
        heights = jax.random.uniform(jax.random.fold_in(jax.random.fold_in(stream_key, 6), axis_at), (shards_of,), jnp.float32, low / len(cuts), high / len(cuts))
        factor_of = factor_of * jnp.repeat(jnp.exp(heights), dims[axis_at] // shards_of).reshape((-1,) + (1,) * (len(dims) - 1 - axis_at))
    return factor_of


def picks_of(rng, rows, number_of, top, lift):
    order = jax.random.permutation(jax.random.fold_in(rng, 1), number_of)
    boost = order
    for power in range(3):
        boost = boost * boost // number_of
    boost = boost * lift // number_of
    tickets = jax.random.randint(jax.random.fold_in(rng, 2), (rows, number_of), 0, 4096) + boost
    sure = jax.random.permutation(jax.random.fold_in(rng, 3), rows)[jnp.arange(number_of) % rows]
    tickets = jnp.where(jnp.arange(rows)[:, None] == sure[None, :], 1 << 14, tickets)
    priority = tickets * number_of + jnp.arange(number_of)
    return lax.top_k(priority.astype(jnp.int32), top)[1].astype(jnp.int32)


def normal_values(own_key, shape, deviation, limit, pieces=(), kind=jnp.bfloat16):
    gain = block_levels(own_key, shape, pieces, -0.22, 0.18) if pieces else 1.0
    array = jax.random.normal(own_key, shape, jnp.float32) * deviation * gain
    return jnp.minimum(jnp.maximum(array, -limit), limit).astype(kind)


def setup_inputs(seed: int = 0, part: int = 0) -> dict:
    arg_keys = jax.random.split(jax.random.key(seed), 6)
    part_splits = jax.random.split(jax.random.fold_in(arg_keys[5], part), 6)
    return {
        "patterns": normal_values(part_splits[0], (POSITIONS, RADII, ANGLES), 1.0, 6.0, ((0, 16),)),
        "templates": normal_values(arg_keys[1], (TEMPLATES, RADII, ANGLES), 1.0, 6.0, ((0, 16),)),
        "radius_bin": touch_ends(jax.random.randint(arg_keys[2], (RADII,), 0, GAINS), jax.random.fold_in(arg_keys[2], 1), 0, GAINS - 1).astype(jnp.int32),
        "radial_gain": jnp.clip(jnp.exp(jax.random.uniform(arg_keys[3], (GAINS,), jnp.float32, math.log(0.25), math.log(4.0))), 0.25, 4.0),
        "orientation": picks_of(arg_keys[4], TEMPLATES, ORIENTS, 1, 0),
    }


def make_tables():
    half = ANGLES // 2
    along = jnp.arange(ANGLES, dtype=jnp.int32)
    modes = jnp.arange(half + 1, dtype=jnp.int32)
    phase = 2.0 * math.pi / ANGLES * (along[:, None] * modes[None, :] % ANGLES).astype(jnp.float32)
    basis = jnp.concatenate([jnp.cos(phase), jnp.sin(phase[:, 1:half])], axis=1).astype(jnp.bfloat16)
    factor_norm = 1.0 / (ANGLES * math.sqrt(RADII * ANGLES))
    mode_weight = jnp.where((modes == 0) | (modes == half), 1.0, 2.0).astype(jnp.float32)
    phase_rows = phase.T
    inverse = jnp.concatenate([mode_weight[:, None] * jnp.cos(phase_rows), -mode_weight[:, None] * jnp.sin(phase_rows)], axis=0)
    return (basis, (inverse * factor_norm).astype(jnp.bfloat16))

def split_modes(spec):
    half = ANGLES // 2
    cos_part = spec[..., :half + 1]
    sin_part = jnp.pad(spec[..., half + 1:], [(0, 0)] * (spec.ndim - 1) + [(1, 1)])
    return (cos_part, sin_part)

def reference(patterns, templates, radius_bin, radial_gain, orientation):
    basis, inverse = make_tables()
    onehot = (radius_bin[:, None] == jnp.arange(GAINS, dtype=jnp.int32)[None, :]).astype(jnp.float32)
    radius_weight = lax.optimization_barrier(jnp.sum(onehot * radial_gain[None, :], axis=1))
    tmpl_spec = jnp.dot(templates.reshape(-1, ANGLES), basis, preferred_element_type=jnp.float32)
    tmpl_spec = tmpl_spec.astype(jnp.bfloat16).reshape(TEMPLATES, RADII, ANGLES)
    tmpl_cos, tmpl_sin = split_modes(tmpl_spec)
    tmpl_cos = tmpl_cos.astype(jnp.float32)
    tmpl_sin = tmpl_sin.astype(jnp.float32)
    inverse_wide = inverse.astype(jnp.float32)
    groups = orientation[:, 0]
    member = groups[:, None] == jnp.arange(ORIENTS, dtype=jnp.int32)[None, :]

    def block(pattern_block):
        spec = jnp.dot(pattern_block.reshape(-1, ANGLES), basis, preferred_element_type=jnp.float32)
        spec = (spec.reshape(POS_DEV, RADII, ANGLES) * radius_weight[None, :, None]).astype(jnp.bfloat16)
        pat_cos, pat_sin = split_modes(spec)
        pat_cos = pat_cos.astype(jnp.float32)
        pat_sin = pat_sin.astype(jnp.float32)
        real_part = jnp.einsum('prk,trk->kpt', pat_cos, tmpl_cos) + jnp.einsum('prk,trk->kpt', pat_sin, tmpl_sin)
        imag_part = jnp.einsum('prk,trk->kpt', pat_cos, tmpl_sin) - jnp.einsum('prk,trk->kpt', pat_sin, tmpl_cos)
        cross = jnp.concatenate([real_part, imag_part], axis=0).astype(jnp.bfloat16).astype(jnp.float32)
        shifted = jnp.einsum('kpt,ks->pts', cross, inverse_wide)
        corr = lax.optimization_barrier(jnp.max(shifted, axis=2))
        best = lax.optimization_barrier(jnp.max(jnp.where(member[None, :, :], corr[:, :, None], -jnp.inf), axis=1))
        return (corr, best)
    corr_blocks, best_blocks = lax.map(block, patterns.reshape(N_SCAN, POS_DEV, RADII, ANGLES))
    corr_map = corr_blocks.reshape(POSITIONS, TEMPLATES)
    best = best_blocks.reshape(POSITIONS, ORIENTS)
    padded = jnp.pad(best, ((1, 1), (0, 0)))
    orient_map = 0.25 * (padded[:-2] + 2.0 * best + padded[2:])
    return (corr_map, orient_map)
```

```python
import math

import jax
import jax.numpy as jnp
import numpy as np
from jax import lax
from jax.experimental import pallas as pl
from jax.experimental.pallas import tpu as pltpu
from jax.sharding import PartitionSpec as P

RADII = 64
ANGLES = 256
HALF = ANGLES // 2
GAINS = 8
TMPL_PER_GROUP = 2
LANES = 128
BLOCK = 32
F32 = jnp.float32
BF16 = jnp.bfloat16
CONTRACT_LAST = (((1,), (1,)), ((), ()))


def make_tables():
    along = np.arange(ANGLES, dtype=np.int32)
    modes = np.arange(HALF + 1, dtype=np.int32)
    scale = np.float32(2.0 * math.pi / ANGLES)
    phase = scale * (along[:, None] * modes[None, :] % ANGLES).astype(np.float32)
    cos, sin = np.cos(phase), np.sin(phase)
    basis = np.concatenate([cos, sin[:, 1:HALF]], axis=1)
    norm = np.float32(1.0 / (ANGLES * math.sqrt(RADII * ANGLES)))
    weight = np.where((modes == 0) | (modes == HALF), 1.0, 2.0).astype(np.float32)
    inv_cos = weight[None, :] * cos * norm
    inv_sin = -weight[None, :] * sin * norm
    inverse = np.concatenate([inv_cos, inv_sin[:, 1:HALF]], axis=1)
    return basis.T.astype(jnp.bfloat16), inverse.astype(jnp.bfloat16)


def template_kernel(tmpl_ref, table_ref, out_ref):
    for t in range(tmpl_ref.shape[0]):
        spec = lax.dot_general(table_ref[...], tmpl_ref[t], CONTRACT_LAST, preferred_element_type=F32)
        out_ref[t] = jnp.concatenate([spec[:HALF], spec[HALF:]], axis=1).astype(BF16)


def pattern_kernel(bin_ref, gain_ref, pat_ref, before_ref, after_ref, table_ref, out_ref, raw_ref, spec_ref):
    count = pat_ref.shape[0]
    zero = jnp.zeros((LANES - count, LANES), F32)

    def put(pos, rows):
        wide = rows.astype(F32)
        raw_ref[0, pl.ds(pos, RADII, stride=LANES), :] = wide[:, :LANES]
        raw_ref[1, pl.ds(pos, RADII, stride=LANES), :] = wide[:, LANES:]

    def fill(r, carry):
        raw_ref[0, pl.ds(r * LANES + count, LANES - count), :] = zero
        raw_ref[1, pl.ds(r * LANES + count, LANES - count), :] = zero
        return carry

    lax.fori_loop(0, RADII, fill, 0, unroll=8)

    def place(p, carry):
        put(p, pat_ref[p])
        return carry

    lax.fori_loop(0, count, place, 0, unroll=8)
    put(count, after_ref[0])
    put(LANES - 1, before_ref[0])

    def step(r, carry):
        begin = pl.multiple_of(r * LANES, LANES)
        rows = jnp.concatenate(
            [raw_ref[0, pl.ds(begin, LANES), :], raw_ref[1, pl.ds(begin, LANES), :]], axis=1
        ).astype(BF16)
        spec = lax.dot_general(table_ref[...], rows, CONTRACT_LAST, preferred_element_type=F32)
        spec = spec * gain_ref[bin_ref[r]]
        spec_ref[pl.ds(r, HALF, stride=2 * RADII), :] = spec[:HALF]
        spec_ref[pl.ds(RADII + r, HALF, stride=2 * RADII), :] = spec[HALF:]
        return carry

    lax.fori_loop(0, RADII, step, 0, unroll=4)

    def narrow(k, carry):
        out_ref[k] = spec_ref[pl.ds(pl.multiple_of(k * LANES, LANES), LANES), :].astype(BF16)
        return carry

    lax.fori_loop(0, HALF, narrow, 0, unroll=8)


def match_kernel(order_ref, tmpl_ref, pat_ref, inv_ref, orient_ref, corr_ref, smooth_ref, side_ref, cross_ref, best_ref):
    total = tmpl_ref.shape[0]
    count = corr_ref.shape[0]
    groups = smooth_ref.shape[1]
    low = lax.broadcasted_iota(jnp.int32, (BLOCK, LANES), 1) < RADII
    sign = jnp.where(lax.broadcasted_iota(jnp.int32, (HALF, LANES), 1) < RADII, 1.0, -1.0).astype(F32)
    for begin in range(0, total, BLOCK):

        def spread(t, carry):
            both = tmpl_ref[order_ref[begin + t]].astype(F32)
            turned = pltpu.roll(both, RADII, 1) * sign
            side_ref[pl.ds(t, HALF, stride=2 * BLOCK), :] = both
            side_ref[pl.ds(BLOCK + t, HALF, stride=2 * BLOCK), :] = turned
            return carry

        lax.fori_loop(0, BLOCK, spread, 0, unroll=4)

        def product(k, left):
            value = jnp.dot(left.astype(BF16), pat_ref[k], preferred_element_type=F32)
            at = k * 2 * BLOCK
            if not isinstance(k, int):
                at = pl.multiple_of(at, 2 * BLOCK)
            cross_ref[pl.ds(at, 2 * BLOCK), :] = value

        edge = side_ref[pl.ds(0, BLOCK), :]
        product(0, jnp.concatenate([jnp.where(low, edge, 0.0), jnp.where(low, 0.0, edge)], axis=0))

        def modes(k, carry):
            product(k, side_ref[pl.ds(pl.multiple_of(k * 2 * BLOCK, 2 * BLOCK), 2 * BLOCK), :])
            return carry

        lax.fori_loop(1, HALF, modes, 0, unroll=8)

        def shifts(t, carry):
            real = cross_ref[pl.ds(t, HALF, stride=2 * BLOCK), :]
            imag = cross_ref[pl.ds(BLOCK + t, HALF, stride=2 * BLOCK), :]
            cross = jnp.concatenate([real, imag], axis=0).astype(BF16)
            shifted = jnp.dot(inv_ref[...], cross, preferred_element_type=F32)
            best_ref[pl.ds(begin + t, 1), :] = jnp.max(shifted, axis=0, keepdims=True)
            return carry

        lax.fori_loop(0, BLOCK, shifts, 0, unroll=4)
    corr = best_ref[...]
    corr_ref[...] = corr.T[:count]
    rows = []
    for g in range(groups):
        rows.append(jnp.max(jnp.where(orient_ref[...] == g, corr, -jnp.inf), axis=0, keepdims=True))
    best = jnp.concatenate(rows, axis=0)
    smooth = 0.25 * (pltpu.roll(best, 1, 1) + 2.0 * best + pltpu.roll(best, LANES - 1, 1))
    smooth_ref[...] = smooth.T[:count]


VMEM = pl.BlockSpec(memory_space=pltpu.VMEM)
SMEM = pl.BlockSpec(memory_space=pltpu.SMEM)


def template_spectra(templates, table):
    return pl.pallas_call(
        template_kernel,
        out_shape=jax.ShapeDtypeStruct((templates.shape[0], HALF, LANES), BF16),
        in_specs=[VMEM] * 2,
        out_specs=VMEM,
        name="template_spectra",
    )(templates, table)


def pattern_spectra(bins, gains, patterns, before, after, table):
    return pl.pallas_call(
        pattern_kernel,
        out_shape=jax.ShapeDtypeStruct((HALF, LANES, LANES), BF16),
        in_specs=[SMEM] * 2 + [VMEM] * 4,
        out_specs=VMEM,
        scratch_shapes=[pltpu.VMEM((2, RADII * LANES, LANES), F32), pltpu.VMEM((HALF * LANES, LANES), F32)],
        name="pattern_spectra",
    )(bins, gains, patterns, before, after, table)


def match(order, spectra, pat_spec, inverse, orientation, count, groups):
    total = spectra.shape[0]
    return pl.pallas_call(
        match_kernel,
        out_shape=(jax.ShapeDtypeStruct((count, total), F32), jax.ShapeDtypeStruct((count, groups), F32)),
        in_specs=[SMEM] + [VMEM] * 4,
        out_specs=(VMEM, VMEM),
        scratch_shapes=[
            pltpu.VMEM((HALF * 2 * BLOCK, LANES), F32),
            pltpu.VMEM((HALF * 2 * BLOCK, LANES), F32),
            pltpu.VMEM((total, LANES), F32),
        ],
        name="match",
    )(order, spectra, pat_spec, inverse, orientation)


def on_device(patterns, templates, radius_bin, radial_gain, orientation):
    table, inverse = make_tables()
    table, inverse = jnp.asarray(table), jnp.asarray(inverse)
    count = patterns.shape[0]
    size = lax.axis_size("scan")
    mine = templates.shape[0]
    total = mine * size
    groups = total // TMPL_PER_GROUP
    own = template_spectra(templates, table)
    up = [(i, i + 1) for i in range(size - 1)]
    down = [(j, i) for i, j in up]
    before = lax.ppermute(patterns[count - 1 :], "scan", up)
    after = lax.ppermute(patterns[:1], "scan", down)
    gathered = own
    held = [0]
    bit = size // 2
    while bit:
        other = lax.ppermute(gathered, "scan", [(i, i ^ bit) for i in range(size)])
        gathered = jnp.concatenate([gathered, other], axis=0)
        held = held + [h ^ bit for h in held]
        bit //= 2
    slot = np.zeros(size, np.int32)
    slot[np.array(held)] = np.arange(size, dtype=np.int32)
    which = jnp.arange(size, dtype=jnp.int32) ^ lax.axis_index("scan").astype(jnp.int32)
    order = (jnp.asarray(slot)[which][:, None] * mine + jnp.arange(mine, dtype=jnp.int32)).reshape(total)
    pat_spec = pattern_spectra(radius_bin, radial_gain, patterns, before, after, table)
    return match(order, gathered, pat_spec, inverse, orientation, count, groups)


def solution(mesh):
    placed = (P(("grp", "scan"), None, None), P("scan", None, None), P(), P(), P())
    return jax.shard_map(
        on_device,
        mesh=mesh,
        in_specs=placed,
        out_specs=(P(("grp", "scan"), None), P(("grp", "scan"), None)),
        check_vma=False,
    )
```

```python
import functools
import math

import jax
import jax.numpy as jnp
import numpy as np
from jax import lax
from jax.experimental import pallas as pl
from jax.experimental.pallas import tpu as pltpu
from jax.sharding import PartitionSpec as P

RADII = 64
ANGLES = 256
HALF = ANGLES // 2
GAINS = 8
TMPL_PER_GROUP = 2
LANES = 128
BLOCK = 32
PER_DEVICE = 2
F32 = jnp.float32
BF16 = jnp.bfloat16
CONTRACT_LAST = (((1,), (1,)), ((), ()))


def make_tables():
    along = np.arange(ANGLES, dtype=np.int32)
    modes = np.arange(HALF + 1, dtype=np.int32)
    scale = np.float32(2.0 * math.pi / ANGLES)
    phase = scale * (along[:, None] * modes[None, :] % ANGLES).astype(np.float32)
    cos, sin = np.cos(phase), np.sin(phase)
    basis = np.concatenate([cos, sin[:, 1:HALF]], axis=1)
    norm = np.float32(1.0 / (ANGLES * math.sqrt(RADII * ANGLES)))
    weight = np.where((modes == 0) | (modes == HALF), 1.0, 2.0).astype(np.float32)
    inv_cos = weight[None, :] * cos * norm
    inv_sin = -weight[None, :] * sin * norm
    inverse = np.concatenate([inv_cos, inv_sin[:, 1:HALF]], axis=1)
    return basis.T.astype(jnp.bfloat16), inverse.astype(jnp.bfloat16)


PITCH = LANES + 8
SIDE = 2 * BLOCK + 8


def pattern_kernel(bin_ref, gain_ref, pat_ref, before_ref, after_ref, table_ref, out_ref, raw_ref, spec_ref, *, first):
    count = pat_ref.shape[0]
    radii = out_ref.shape[1] // 2
    pitch = 2 * radii + 8
    zero = jnp.zeros((LANES - count, LANES), F32)

    def put(pos, rows):
        wide = rows.astype(F32)
        raw_ref[0, pl.ds(pos, radii, stride=PITCH), :] = wide[:, :LANES]
        raw_ref[1, pl.ds(pos, radii, stride=PITCH), :] = wide[:, LANES:]

    for r in range(radii):
        raw_ref[0, pl.ds(r * PITCH + count, LANES - count), :] = zero
        raw_ref[1, pl.ds(r * PITCH + count, LANES - count), :] = zero

    def place(p, carry):
        put(p, pat_ref[p, pl.ds(first, radii)])
        return carry

    lax.fori_loop(0, count, place, 0, unroll=16)
    put(count, after_ref[0, pl.ds(first, radii)])
    put(LANES - 1, before_ref[0, pl.ds(first, radii)])

    def step(r, carry):
        begin = pl.multiple_of(r * PITCH, 8)
        rows = jnp.concatenate(
            [raw_ref[0, pl.ds(begin, LANES), :], raw_ref[1, pl.ds(begin, LANES), :]], axis=1
        ).astype(BF16)
        spec = lax.dot_general(table_ref[...], rows, CONTRACT_LAST, preferred_element_type=F32)
        spec = spec * gain_ref[bin_ref[first + r]]
        spec_ref[pl.ds(r, HALF, stride=pitch), :] = spec[:HALF]
        spec_ref[pl.ds(radii + r, HALF, stride=pitch), :] = spec[HALF:]
        return carry

    lax.fori_loop(0, radii, step, 0, unroll=16)

    def narrow(k, carry):
        out_ref[k] = spec_ref[pl.ds(pl.multiple_of(k * pitch, 8), 2 * radii), :].astype(BF16)
        return carry

    lax.fori_loop(0, HALF, narrow, 0, unroll=16)


def match_kernel(
    index_ref, orient_ref, tmpl_ref, low_ref, high_ref, table_ref, inv_ref, corr_ref, smooth_ref, side_ref, cross_ref, best_ref
):
    total = tmpl_ref.shape[0]
    count = corr_ref.shape[1]
    bits = (total // PER_DEVICE).bit_length() - 1
    best_ref[...] = jnp.full(best_ref.shape, -jnp.inf, F32)
    low = lax.broadcasted_iota(jnp.int32, (HALF, LANES), 1) < RADII
    low_edge = lax.broadcasted_iota(jnp.int32, (BLOCK, LANES), 1) < RADII

    def chunk(begin):
        for t in range(0, BLOCK, 2):
            pair = tmpl_ref[pl.ds(begin + t, 2)].reshape(2 * RADII, ANGLES)
            spec = lax.dot_general(table_ref[...], pair, CONTRACT_LAST, preferred_element_type=F32)
            cos, sin = spec[:HALF], spec[HALF:]
            turned_cos, turned_sin = pltpu.roll(cos, RADII, 1), pltpu.roll(sin, RADII, 1)
            side_ref[pl.ds(t, HALF, stride=SIDE), :] = jnp.where(low, cos, turned_sin)
            side_ref[pl.ds(t + 1, HALF, stride=SIDE), :] = jnp.where(low, turned_cos, sin)
            side_ref[pl.ds(BLOCK + t, HALF, stride=SIDE), :] = jnp.where(low, sin, -turned_cos)
            side_ref[pl.ds(BLOCK + t + 1, HALF, stride=SIDE), :] = jnp.where(low, turned_sin, -cos)
        for k in range(HALF):
            if k:
                left = side_ref[pl.ds(k * SIDE, 2 * BLOCK), :]
            else:
                edge = side_ref[pl.ds(0, BLOCK), :]
                left = jnp.concatenate([jnp.where(low_edge, edge, 0.0), jnp.where(low_edge, 0.0, edge)], axis=0)
            lower, upper = low_ref[k], high_ref[k]
            half = RADII // 2
            right = jnp.concatenate([lower[:half], upper[:half], lower[half:], upper[half:]], axis=0)
            cross_ref[pl.ds(k * SIDE, 2 * BLOCK), :] = jnp.dot(left.astype(BF16), right, preferred_element_type=F32)
        rows = []
        for t in range(BLOCK):
            real = cross_ref[pl.ds(t, HALF, stride=SIDE), :]
            imag = cross_ref[pl.ds(BLOCK + t, HALF, stride=SIDE), :]
            cross = jnp.concatenate([real, imag], axis=0).astype(BF16)
            shifted = jnp.dot(inv_ref[...], cross, preferred_element_type=F32)
            rows.append(jnp.max(shifted, axis=0, keepdims=True))
        for t in range(BLOCK):
            place = begin + t
            held = place // PER_DEVICE
            device = index_ref[0]
            for b in range(bits):
                device = device ^ (((held >> b) & 1) << (bits - 1 - b))
            where = device * PER_DEVICE + place % PER_DEVICE
            corr_ref[pl.ds(where, 1), :] = rows[t][:, :count]
            group = orient_ref[where]
            best_ref[pl.ds(group, 1), :] = jnp.maximum(best_ref[pl.ds(group, 1), :], rows[t])

    chunk(0)
    if total > BLOCK:

        def more(i, carry):
            chunk(i * BLOCK)
            return carry

        lax.fori_loop(1, total // BLOCK, more, 0)
    best = best_ref[...]
    smooth = 0.25 * (pltpu.roll(best, 1, 1) + 2.0 * best + pltpu.roll(best, LANES - 1, 1))
    smooth_ref[...] = smooth[:, :count]


VMEM = pl.BlockSpec(memory_space=pltpu.VMEM)
SMEM = pl.BlockSpec(memory_space=pltpu.SMEM)
HBM = pl.BlockSpec(memory_space=pl.ANY)


def pattern_spectra(first, radii, bins, gains, patterns, before, after, table):
    return pl.pallas_call(
        functools.partial(pattern_kernel, first=first),
        out_shape=jax.ShapeDtypeStruct((HALF, 2 * radii, LANES), BF16),
        in_specs=[SMEM] * 2 + [VMEM] * 4,
        out_specs=VMEM,
        scratch_shapes=[
            pltpu.VMEM((2, radii * PITCH, LANES), F32),
            pltpu.VMEM((HALF * (2 * radii + 8), LANES), F32),
        ],
        compiler_params=pltpu.CompilerParams(vmem_limit_bytes=24 << 20),
        name="pattern_spectra",
    )(bins, gains, patterns, before, after, table)


def match(index, orientation, templates, lower, upper, table, inverse, count, groups):
    total = templates.shape[0]
    return pl.pallas_call(
        match_kernel,
        out_shape=(jax.ShapeDtypeStruct((total, count), F32), jax.ShapeDtypeStruct((groups, count), F32)),
        in_specs=[SMEM] * 2 + [VMEM] * 5,
        out_specs=(VMEM, VMEM),
        scratch_shapes=[
            pltpu.VMEM((HALF * SIDE, LANES), F32),
            pltpu.VMEM((HALF * SIDE, LANES), F32),
            pltpu.VMEM((groups, LANES), F32),
        ],
        compiler_params=pltpu.CompilerParams(vmem_limit_bytes=32 << 20),
        name="match",
    )(index, orientation, templates, lower, upper, table, inverse)


def on_device(patterns, templates, radius_bin, radial_gain, orientation):
    table, inverse = make_tables()
    table, inverse = jnp.asarray(table), jnp.asarray(inverse)
    count = patterns.shape[0]
    size = lax.axis_size("scan")
    mine = templates.shape[0]
    groups = mine * size // TMPL_PER_GROUP
    up = [(i, i + 1) for i in range(size - 1)]
    down = [(j, i) for i, j in up]
    steps = [1 << b for b in reversed(range(size.bit_length() - 1))]
    before = lax.ppermute(patterns[count - 1 :], "scan", up)
    after = lax.ppermute(patterns[:1], "scan", down)
    gathered = templates
    halves = []
    for number, bit in enumerate(steps):
        length = gathered.shape[0]
        other = lax.ppermute(gathered, "scan", [(i, i ^ bit) for i in range(size)])
        room = lax.optimization_barrier(
            lax.dynamic_update_slice(jnp.zeros((2 * length,) + gathered.shape[1:], BF16), gathered, (0, 0, 0))
        )
        gathered = lax.dynamic_update_slice(room, other, (length, 0, 0))
        if number == 0:
            gathered, before, after = lax.optimization_barrier((gathered, before, after))
        elif number <= 2:
            half = pattern_spectra(
                (number - 1) * (RADII // 2), RADII // 2, radius_bin, radial_gain, patterns, before, after, table
            )
            gathered, half, before, after = lax.optimization_barrier((gathered, half, before, after))
            halves.append(half)
        else:
            gathered = lax.optimization_barrier(gathered)
    index = lax.axis_index("scan").astype(jnp.int32).reshape(1)
    corr, smooth = match(index, orientation.reshape(-1), gathered, *halves, table, inverse, count, groups)
    return corr.T, smooth.T


def solution(mesh):
    placed = (P(("grp", "scan"), None, None), P("scan", None, None), P(), P(), P())
    return jax.shard_map(
        on_device,
        mesh=mesh,
        in_specs=placed,
        out_specs=(P(("grp", "scan"), None), P(("grp", "scan"), None)),
        check_vma=False,
    )
```

```python
import functools
import math

import jax
import jax.numpy as jnp
import numpy as np
from jax import lax
from jax.experimental import pallas as pl
from jax.experimental.pallas import tpu as pltpu
from jax.sharding import PartitionSpec as P

RADII = 64
ANGLES = 256
HALF = ANGLES // 2
GAINS = 8
TMPL_PER_GROUP = 2
LANES = 128
BLOCK = 32
ROWS = 16
PER_DEVICE = 2
F32 = jnp.float32
BF16 = jnp.bfloat16
CONTRACT_LAST = (((1,), (1,)), ((), ()))


def make_tables():
    along = np.arange(ANGLES, dtype=np.int32)
    modes = np.arange(HALF + 1, dtype=np.int32)
    scale = np.float32(2.0 * math.pi / ANGLES)
    phase = scale * (along[:, None] * modes[None, :] % ANGLES).astype(np.float32)
    cos, sin = np.cos(phase), np.sin(phase)
    basis = np.concatenate([cos, sin[:, 1:HALF]], axis=1)
    norm = np.float32(1.0 / (ANGLES * math.sqrt(RADII * ANGLES)))
    weight = np.where((modes == 0) | (modes == HALF), 1.0, 2.0).astype(np.float32)
    inv_cos = weight[None, :] * cos * norm
    inv_sin = -weight[None, :] * sin * norm
    inverse = np.concatenate([inv_cos, inv_sin[:, 1:HALF]], axis=1)
    return basis.T.astype(jnp.bfloat16), inverse.astype(jnp.bfloat16)


PITCH = LANES + 8
SIDE = 2 * BLOCK + 8


def arrange_kernel(pat_hbm, tmpl_hbm, table_hbm, out_ref, own_ref, table_ref, pat_ref, raw_ref, sem, side_sem):
    chunks = pat_ref.shape[0] // ROWS

    def fetch(c):
        part = pl.ds(c * ROWS, ROWS)
        return pltpu.make_async_copy(pat_hbm.at[part], pat_ref.at[part], sem.at[c])

    sides = [
        pltpu.make_async_copy(tmpl_hbm, own_ref, side_sem.at[0]),
        pltpu.make_async_copy(table_hbm, table_ref, side_sem.at[1]),
    ]
    for c in range(chunks):
        fetch(c).start()
    for copy in sides:
        copy.start()
    for c in range(chunks):
        fetch(c).wait()
        for p in range(ROWS):
            wide = pat_ref[c * ROWS + p].astype(F32)
            raw_ref[c % 2, 0, pl.ds(p, RADII, stride=ROWS + 8), :] = wide[:, :LANES]
            raw_ref[c % 2, 1, pl.ds(p, RADII, stride=ROWS + 8), :] = wide[:, LANES:]
        for r in range(RADII):
            at = pl.ds(r * (ROWS + 8), ROWS)
            out_ref[r, pl.ds(c * ROWS, ROWS), :] = jnp.concatenate(
                [raw_ref[c % 2, 0, at, :], raw_ref[c % 2, 1, at, :]], axis=1
            ).astype(BF16)
    for copy in sides:
        copy.wait()


def pattern_kernel(bin_ref, gain_ref, rows_ref, inner_ref, outer_ref, table_ref, out_ref, edge_ref, weight_ref, spec_ref):
    count = rows_ref.shape[1]
    spare = LANES - count
    pitch = spare + 8
    even = lax.axis_index("scan") % 2 == 0
    edge_ref[...] = jnp.zeros(edge_ref.shape, F32)
    inner, outer = inner_ref[0].astype(F32), outer_ref[0].astype(F32)
    for at, wide in ((0, jnp.where(even, inner, outer)), (spare - 1, jnp.where(even, outer, inner))):
        edge_ref[0, pl.ds(at, RADII, stride=pitch), :] = wide[:, :LANES]
        edge_ref[1, pl.ds(at, RADII, stride=pitch), :] = wide[:, LANES:]
    for r in range(RADII):
        weight_ref[pl.ds(r, 1), :] = jnp.full((1, LANES), gain_ref[bin_ref[r]], F32)
    for r in range(RADII):
        at = pl.ds(r * pitch, spare)
        edge = jnp.concatenate([edge_ref[0, at, :], edge_ref[1, at, :]], axis=1).astype(BF16)
        rows = jnp.concatenate([rows_ref[r], edge], axis=0)
        spec = lax.dot_general(table_ref[...], rows, CONTRACT_LAST, preferred_element_type=F32)
        spec = spec * weight_ref[pl.ds(r, 1), :]
        spec_ref[pl.ds(r, HALF, stride=PITCH), :] = spec[:HALF]
        spec_ref[pl.ds(RADII + r, HALF, stride=PITCH), :] = spec[HALF:]
    for k in range(HALF):
        out_ref[k] = spec_ref[pl.ds(k * PITCH, LANES), :].astype(BF16)


def match_kernel(orient_ref, pat_ref, table_ref, inv_ref, *refs, held):
    parts = refs[: len(held)]
    corr_ref, smooth_ref, side_ref, cross_ref, best_ref = refs[len(held) :]
    count = corr_ref.shape[1]
    index = lax.axis_index("scan")
    blocks = [(part, i, mask) for part, masks in zip(parts, held) for i, mask in enumerate(masks)]
    best_ref[...] = jnp.full(best_ref.shape, -jnp.inf, F32)
    low = lax.broadcasted_iota(jnp.int32, (HALF, LANES), 1) < RADII
    low_edge = lax.broadcasted_iota(jnp.int32, (BLOCK, LANES), 1) < RADII
    for begin in range(0, len(blocks), BLOCK // PER_DEVICE):
        chunk = blocks[begin : begin + BLOCK // PER_DEVICE]
        for number, (part, i, _) in enumerate(chunk):
            t = number * PER_DEVICE
            pair = part[pl.ds(i * PER_DEVICE, PER_DEVICE)].reshape(PER_DEVICE * RADII, ANGLES)
            spec = lax.dot_general(table_ref[...], pair, CONTRACT_LAST, preferred_element_type=F32)
            cos, sin = spec[:HALF], spec[HALF:]
            turned_cos, turned_sin = pltpu.roll(cos, RADII, 1), pltpu.roll(sin, RADII, 1)
            side_ref[pl.ds(t, HALF, stride=SIDE), :] = jnp.where(low, cos, turned_sin)
            side_ref[pl.ds(t + 1, HALF, stride=SIDE), :] = jnp.where(low, turned_cos, sin)
            side_ref[pl.ds(BLOCK + t, HALF, stride=SIDE), :] = jnp.where(low, sin, -turned_cos)
            side_ref[pl.ds(BLOCK + t + 1, HALF, stride=SIDE), :] = jnp.where(low, turned_sin, -cos)
        for k in range(HALF):
            if k:
                left = side_ref[pl.ds(k * SIDE, 2 * BLOCK), :]
            else:
                edge = side_ref[pl.ds(0, BLOCK), :]
                left = jnp.concatenate([jnp.where(low_edge, edge, 0.0), jnp.where(low_edge, 0.0, edge)], axis=0)
            cross_ref[pl.ds(k * SIDE, 2 * BLOCK), :] = jnp.dot(
                left.astype(BF16), pat_ref[k], preferred_element_type=F32
            )
        rows = []
        for t in range(0, len(chunk) * PER_DEVICE, 2):
            cross = [
                jnp.concatenate(
                    [cross_ref[pl.ds(u, HALF, stride=SIDE), :], cross_ref[pl.ds(BLOCK + u, HALF, stride=SIDE), :]], axis=0
                ).astype(BF16)
                for u in (t, t + 1)
            ]
            shifted = jnp.dot(inv_ref[...], jnp.concatenate(cross, axis=1), preferred_element_type=F32)
            top = jnp.max(shifted, axis=0, keepdims=True)
            rows += [top[:, :LANES], top[:, LANES:]]
        for number, (_, _, mask) in enumerate(chunk):
            for e in range(PER_DEVICE):
                row = rows[number * PER_DEVICE + e]
                where = (index ^ mask) * PER_DEVICE + e
                corr_ref[pl.ds(where, 1), :] = row[:, :count]
                group = orient_ref[where]
                best_ref[pl.ds(group, 1), :] = jnp.maximum(best_ref[pl.ds(group, 1), :], row)
    best = best_ref[...]
    smooth = 0.25 * (pltpu.roll(best, 1, 1) + 2.0 * best + pltpu.roll(best, LANES - 1, 1))
    smooth_ref[...] = smooth[:, :count]


VMEM = pl.BlockSpec(memory_space=pltpu.VMEM)
SMEM = pl.BlockSpec(memory_space=pltpu.SMEM)
HBM = pl.BlockSpec(memory_space=pltpu.HBM)


def arrange(patterns, templates, table):
    count = patterns.shape[0]
    args = (patterns, templates, table)
    return pl.pallas_call(
        arrange_kernel,
        out_shape=(
            jax.ShapeDtypeStruct((RADII, count, ANGLES), BF16),
            jax.ShapeDtypeStruct(templates.shape, BF16),
            jax.ShapeDtypeStruct(table.shape, BF16),
        ),
        in_specs=[HBM] * 3,
        out_specs=(VMEM,) * 3,
        scratch_shapes=[
            pltpu.VMEM(patterns.shape, BF16),
            pltpu.VMEM((2, 2, RADII * (ROWS + 8), LANES), F32),
            pltpu.SemaphoreType.DMA((count // ROWS,)),
            pltpu.SemaphoreType.DMA((2,)),
        ],
        compiler_params=pltpu.CompilerParams(vmem_limit_bytes=16 << 20),
        name="arrange",
    )(*(pltpu.with_memory_space_constraint(x, pltpu.HBM) for x in args))


def pattern_spectra(bins, gains, rows, inner, outer, table):
    spare = LANES - rows.shape[1]
    return pl.pallas_call(
        pattern_kernel,
        out_shape=jax.ShapeDtypeStruct((HALF, LANES, LANES), BF16),
        in_specs=[SMEM] * 2 + [VMEM] * 4,
        out_specs=VMEM,
        scratch_shapes=[
            pltpu.VMEM((2, RADII * (spare + 8), LANES), F32),
            pltpu.VMEM((RADII, LANES), F32),
            pltpu.VMEM((HALF * PITCH, LANES), F32),
        ],
        compiler_params=pltpu.CompilerParams(vmem_limit_bytes=16 << 20),
        name="pattern_spectra",
    )(bins, gains, rows, inner, outer, table)


def match(orientation, pat_spec, table, inverse, parts, held, count, groups):
    total = orientation.shape[0]
    return pl.pallas_call(
        functools.partial(match_kernel, held=held),
        out_shape=(jax.ShapeDtypeStruct((total, count), F32), jax.ShapeDtypeStruct((groups, count), F32)),
        in_specs=[SMEM] + [VMEM] * (3 + len(parts)),
        out_specs=(VMEM, VMEM),
        scratch_shapes=[
            pltpu.VMEM((HALF * SIDE, LANES), F32),
            pltpu.VMEM((HALF * SIDE, LANES), F32),
            pltpu.VMEM((groups, LANES), F32),
        ],
        compiler_params=pltpu.CompilerParams(vmem_limit_bytes=24 << 20),
        name="match",
    )(orientation, pat_spec, table, inverse, *parts)


def swap_edges(patterns, size):
    even = lax.axis_index("scan") % 2 == 0
    leading, last = patterns[:1], patterns[patterns.shape[0] - 1 :]
    inner, outer = jnp.where(even, last, leading), jnp.where(even, leading, last)
    inner = lax.ppermute(inner, "scan", [(i, i ^ 1) for i in range(size)])
    pairs = [(i, i + 1) for i in range(1, size - 1, 2)]
    outer = lax.ppermute(outer, "scan", pairs + [(j, i) for i, j in pairs])
    return inner, outer


def on_device(patterns, templates, radius_bin, radial_gain, orientation):
    table, inverse = make_tables()
    table, inverse = jnp.asarray(table), jnp.asarray(inverse)
    count = patterns.shape[0]
    size = lax.axis_size("scan")
    groups = templates.shape[0] * size // TMPL_PER_GROUP
    bits = [1 << b for b in reversed(range(size.bit_length() - 1))]
    far, near, middle, core = bits[0], bits[1], bits[2:-1], bits[-1]

    def send(part, mask):
        return lax.ppermute(part, "scan", [(i, i ^ mask) for i in range(size)])

    masks = [0, far, far ^ near, near]
    came = [send(templates, mask) for mask in masks[1:]]
    inner, outer = swap_edges(patterns, size)
    rows, own, table = arrange(patterns, templates, table)
    came, rows, own, table, inner, outer = lax.optimization_barrier((came, rows, own, table, inner, outer))
    part = lax.optimization_barrier(jnp.concatenate([own] + came, axis=0))
    parts, held = [part], [masks]
    for mask in middle:
        if mask != middle[0]:
            parts, held = [jnp.concatenate(parts, axis=0)], [held[0] + held[1]]
        parts, held = parts + [send(parts[0], mask)], held + [[m ^ mask for m in held[0]]]
    pat_spec = pattern_spectra(radius_bin, radial_gain, rows, inner, outer, table)
    crossed = send(parts[0], core)
    last, pat_spec = lax.optimization_barrier((parts[-1], pat_spec))
    parts = [parts[0], last, crossed, send(last, core)]
    held = held + [[m ^ core for m in masks] for masks in held]
    corr, smooth = match(orientation.reshape(-1), pat_spec, table, inverse, parts, held, count, groups)
    return corr.T, smooth.T


def solution(mesh):
    placed = (P(("grp", "scan"), None, None), P("scan", None, None), P(), P(), P())
    return jax.shard_map(
        on_device,
        mesh=mesh,
        in_specs=placed,
        out_specs=(P(("grp", "scan"), None), P(("grp", "scan"), None)),
        check_vma=False,
    )
```

```python
import functools
import math

import jax
import jax.numpy as jnp
import numpy as np
from jax import lax
from jax.experimental import pallas as pl
from jax.experimental.pallas import tpu as pltpu
from jax.sharding import PartitionSpec as P

RADII = 64
ANGLES = 256
HALF = ANGLES // 2
GAINS = 8
TMPL_PER_GROUP = 2
LANES = 128
BLOCK = 16
ROWS = 16
PER_DEVICE = 2
F32 = jnp.float32
BF16 = jnp.bfloat16
CONTRACT_LAST = (((1,), (1,)), ((), ()))


def make_tables():
    along = np.arange(ANGLES, dtype=np.int32)
    modes = np.arange(HALF + 1, dtype=np.int32)
    scale = np.float32(2.0 * math.pi / ANGLES)
    phase = scale * (along[:, None] * modes[None, :] % ANGLES).astype(np.float32)
    cos, sin = np.cos(phase), np.sin(phase)
    basis = np.concatenate([cos, sin[:, 1:HALF]], axis=1)
    norm = np.float32(1.0 / (ANGLES * math.sqrt(RADII * ANGLES)))
    weight = np.where((modes == 0) | (modes == HALF), 1.0, 2.0).astype(np.float32)
    inv_cos = weight[None, :] * cos * norm
    inv_sin = -weight[None, :] * sin * norm
    inverse = np.concatenate([inv_cos, inv_sin[:, 1:HALF]], axis=1)
    return basis.T.astype(jnp.bfloat16), inverse.astype(jnp.bfloat16)


PITCH = LANES + 8
SIDE = 2 * BLOCK + 8


def arrange_kernel(pat_hbm, tmpl_hbm, table_hbm, out_ref, own_ref, table_ref, pat_ref, raw_ref, sem, side_sem):
    chunks = pat_ref.shape[0] // ROWS

    def fetch(c):
        part = pl.ds(c * ROWS, ROWS)
        return pltpu.make_async_copy(pat_hbm.at[part], pat_ref.at[part], sem.at[c])

    sides = [
        pltpu.make_async_copy(tmpl_hbm, own_ref, side_sem.at[0]),
        pltpu.make_async_copy(table_hbm, table_ref, side_sem.at[1]),
    ]
    for c in range(chunks):
        fetch(c).start()
    for copy in sides:
        copy.start()
    for c in range(chunks):
        fetch(c).wait()
        for p in range(ROWS):
            wide = pat_ref[c * ROWS + p].astype(F32)
            raw_ref[c % 2, 0, pl.ds(p, RADII, stride=ROWS + 8), :] = wide[:, :LANES]
            raw_ref[c % 2, 1, pl.ds(p, RADII, stride=ROWS + 8), :] = wide[:, LANES:]
        for r in range(RADII):
            at = pl.ds(r * (ROWS + 8), ROWS)
            out_ref[r, pl.ds(c * ROWS, ROWS), :] = jnp.concatenate(
                [raw_ref[c % 2, 0, at, :], raw_ref[c % 2, 1, at, :]], axis=1
            ).astype(BF16)
    for copy in sides:
        copy.wait()


def pattern_kernel(bin_ref, gain_ref, rows_ref, inner_ref, outer_ref, table_ref, out_ref, edge_ref, weight_ref, spec_ref):
    count = rows_ref.shape[1]
    spare = LANES - count
    pitch = spare + 8
    even = lax.axis_index("scan") % 2 == 0
    edge_ref[...] = jnp.zeros(edge_ref.shape, F32)
    inner, outer = inner_ref[0].astype(F32), outer_ref[0].astype(F32)
    for at, wide in ((0, jnp.where(even, inner, outer)), (spare - 1, jnp.where(even, outer, inner))):
        edge_ref[0, pl.ds(at, RADII, stride=pitch), :] = wide[:, :LANES]
        edge_ref[1, pl.ds(at, RADII, stride=pitch), :] = wide[:, LANES:]
    for r in range(RADII):
        weight_ref[pl.ds(r, 1), :] = jnp.full((1, LANES), gain_ref[bin_ref[r]], F32)
    for r in range(0, RADII, 2):
        rows = []
        for u in (r, r + 1):
            at = pl.ds(u * pitch, spare)
            rows += [rows_ref[u], jnp.concatenate([edge_ref[0, at, :], edge_ref[1, at, :]], axis=1).astype(BF16)]
        spec = lax.dot_general(
            table_ref[...], jnp.concatenate(rows, axis=0), CONTRACT_LAST, preferred_element_type=F32
        )
        for u in (r, r + 1):
            one = spec[:, (u - r) * LANES : (u - r + 1) * LANES] * weight_ref[pl.ds(u, 1), :]
            spec_ref[pl.ds(u, HALF, stride=PITCH), :] = one[:HALF]
            spec_ref[pl.ds(RADII + u, HALF, stride=PITCH), :] = one[HALF:]
    for k in range(HALF):
        out_ref[k] = spec_ref[pl.ds(k * PITCH, LANES), :].astype(BF16)


def match_kernel(orient_ref, pat_ref, table_ref, inv_ref, *refs, held, more):
    parts, refs = refs[: len(held)], refs[len(held) :]
    if more:
        corr_ref, best_ref, side_ref, cross_ref = refs
        best_ref[...] = jnp.full(best_ref.shape, -jnp.inf, F32)
    else:
        corr_in, best_in, corr_ref, smooth_ref, side_ref, cross_ref, best_ref = refs
        corr_ref[...] = corr_in[...]
        best_ref[...] = best_in[...]
    count = corr_ref.shape[1]
    index = lax.axis_index("scan")
    blocks = [(part, i, mask) for part, masks in zip(parts, held) for i, mask in enumerate(masks)]
    low = lax.broadcasted_iota(jnp.int32, (HALF, LANES), 1) < RADII
    low_edge = lax.broadcasted_iota(jnp.int32, (BLOCK, LANES), 1) < RADII
    for begin in range(0, len(blocks), BLOCK // PER_DEVICE):
        chunk = blocks[begin : begin + BLOCK // PER_DEVICE]
        for number in range(0, len(chunk), 2):
            (part, i, _), (other, j, _) = chunk[number : number + 2]
            raw = jnp.concatenate([part[pl.ds(i * PER_DEVICE, PER_DEVICE)], other[pl.ds(j * PER_DEVICE, PER_DEVICE)]])
            raw = raw.reshape(2 * PER_DEVICE * RADII, ANGLES)
            both = lax.dot_general(table_ref[...], raw, CONTRACT_LAST, preferred_element_type=F32)
            for u in (0, 1):
                t = (number + u) * PER_DEVICE
                spec = both[:, u * LANES : (u + 1) * LANES]
                cos, sin = spec[:HALF], spec[HALF:]
                turned_cos, turned_sin = pltpu.roll(cos, RADII, 1), pltpu.roll(sin, RADII, 1)
                side_ref[pl.ds(t, HALF, stride=SIDE), :] = jnp.where(low, cos, turned_sin)
                side_ref[pl.ds(t + 1, HALF, stride=SIDE), :] = jnp.where(low, turned_cos, sin)
                side_ref[pl.ds(BLOCK + t, HALF, stride=SIDE), :] = jnp.where(low, sin, -turned_cos)
                side_ref[pl.ds(BLOCK + t + 1, HALF, stride=SIDE), :] = jnp.where(low, turned_sin, -cos)
        for k in range(HALF):
            if k:
                left = side_ref[pl.ds(k * SIDE, 2 * BLOCK), :]
            else:
                edge = side_ref[pl.ds(0, BLOCK), :]
                left = jnp.concatenate([jnp.where(low_edge, edge, 0.0), jnp.where(low_edge, 0.0, edge)], axis=0)
            cross_ref[pl.ds(k * SIDE, 2 * BLOCK), :] = jnp.dot(
                left.astype(BF16), pat_ref[k], preferred_element_type=F32
            )
        rows = []
        for t in range(0, len(chunk) * PER_DEVICE, 2):
            cross = [
                jnp.concatenate(
                    [cross_ref[pl.ds(u, HALF, stride=SIDE), :], cross_ref[pl.ds(BLOCK + u, HALF, stride=SIDE), :]], axis=0
                ).astype(BF16)
                for u in (t, t + 1)
            ]
            shifted = jnp.dot(inv_ref[...], jnp.concatenate(cross, axis=1), preferred_element_type=F32)
            top = jnp.max(shifted, axis=0, keepdims=True)
            rows += [top[:, :LANES], top[:, LANES:]]
        for number, (_, _, mask) in enumerate(chunk):
            for e in range(PER_DEVICE):
                row = rows[number * PER_DEVICE + e]
                where = (index ^ mask) * PER_DEVICE + e
                corr_ref[pl.ds(where, 1), :] = row[:, :count]
                group = orient_ref[where]
                best_ref[pl.ds(group, 1), :] = jnp.maximum(best_ref[pl.ds(group, 1), :], row)
    if more:
        return
    best = best_ref[...]
    smooth = 0.25 * (pltpu.roll(best, 1, 1) + 2.0 * best + pltpu.roll(best, LANES - 1, 1))
    smooth_ref[...] = smooth[:, :count]


VMEM = pl.BlockSpec(memory_space=pltpu.VMEM)
SMEM = pl.BlockSpec(memory_space=pltpu.SMEM)
HBM = pl.BlockSpec(memory_space=pltpu.HBM)


def arrange(patterns, templates, table):
    count = patterns.shape[0]
    args = (patterns, templates, table)
    return pl.pallas_call(
        arrange_kernel,
        out_shape=(
            jax.ShapeDtypeStruct((RADII, count, ANGLES), BF16),
            jax.ShapeDtypeStruct(templates.shape, BF16),
            jax.ShapeDtypeStruct(table.shape, BF16),
        ),
        in_specs=[HBM] * 3,
        out_specs=(VMEM,) * 3,
        scratch_shapes=[
            pltpu.VMEM(patterns.shape, BF16),
            pltpu.VMEM((2, 2, RADII * (ROWS + 8), LANES), F32),
            pltpu.SemaphoreType.DMA((count // ROWS,)),
            pltpu.SemaphoreType.DMA((2,)),
        ],
        compiler_params=pltpu.CompilerParams(vmem_limit_bytes=16 << 20),
        name="arrange",
    )(*(pltpu.with_memory_space_constraint(x, pltpu.HBM) for x in args))


def pattern_spectra(bins, gains, rows, inner, outer, table):
    spare = LANES - rows.shape[1]
    return pl.pallas_call(
        pattern_kernel,
        out_shape=jax.ShapeDtypeStruct((HALF, LANES, LANES), BF16),
        in_specs=[SMEM] * 2 + [VMEM] * 4,
        out_specs=VMEM,
        scratch_shapes=[
            pltpu.VMEM((2, RADII * (spare + 8), LANES), F32),
            pltpu.VMEM((RADII, LANES), F32),
            pltpu.VMEM((HALF * PITCH, LANES), F32),
        ],
        compiler_params=pltpu.CompilerParams(vmem_limit_bytes=16 << 20),
        name="pattern_spectra",
    )(bins, gains, rows, inner, outer, table)


def match(orientation, pat_spec, table, inverse, parts, held, carry, count, groups):
    corr = jax.ShapeDtypeStruct((orientation.shape[0], count), F32)
    best = pltpu.VMEM((groups, LANES), F32)
    scratch = [pltpu.VMEM((HALF * SIDE, LANES), F32), pltpu.VMEM((HALF * SIDE, LANES), F32)]
    second = jax.ShapeDtypeStruct((groups, count if carry else LANES), F32)
    return pl.pallas_call(
        functools.partial(match_kernel, held=held, more=not carry),
        out_shape=(corr, second),
        in_specs=[SMEM] + [VMEM] * (3 + len(parts) + len(carry)),
        out_specs=(VMEM, VMEM),
        scratch_shapes=scratch + [best] * bool(carry),
        compiler_params=pltpu.CompilerParams(vmem_limit_bytes=16 << 20),
        name="match",
    )(orientation, pat_spec, table, inverse, *parts, *carry)


def on_device(patterns, templates, radius_bin, radial_gain, orientation):
    table, inverse = make_tables()
    table, inverse = jnp.asarray(table), jnp.asarray(inverse)
    count = patterns.shape[0]
    size = lax.axis_size("scan")
    groups = templates.shape[0] * size // TMPL_PER_GROUP
    orientation = orientation.reshape(-1)
    bits = [1 << b for b in reversed(range(size.bit_length() - 1))]
    far, near, middle, core = bits[0], bits[1], bits[2:-1], bits[-1]

    def send(part, mask):
        return lax.ppermute(part, "scan", [(i, i ^ mask) for i in range(size)])

    masks = [0, far, far ^ near, near]
    came = [send(templates, mask) for mask in masks[1:]]
    even = lax.axis_index("scan") % 2 == 0
    leading, last = patterns[:1], patterns[count - 1 :]
    inner, outer = jnp.where(even, last, leading), jnp.where(even, leading, last)
    pairs = [(i, i + 1) for i in range(1, size - 1, 2)]
    inner = send(inner, 1)
    outer = lax.ppermute(outer, "scan", pairs + [(j, i) for i, j in pairs])
    rows, own, table = arrange(patterns, templates, table)
    came, rows, own, table, inner, outer = lax.optimization_barrier((came, rows, own, table, inner, outer))
    part = lax.optimization_barrier(jnp.concatenate([own] + came, axis=0))
    parts, held = [part], [masks]
    for mask in middle:
        if mask != middle[0]:
            parts, held = [jnp.concatenate(parts, axis=0)], [held[0] + held[1]]
        parts, held = parts + [send(parts[0], mask)], held + [[m ^ mask for m in held[0]]]
    pat_spec = pattern_spectra(radius_bin, radial_gain, rows, inner, outer, table)
    crossed = [[m ^ core for m in masks] for masks in held]
    early = [parts[0], send(parts[0], core)]
    carry = match(orientation, pat_spec, table, inverse, early, [held[0], crossed[0]], [], count, groups)
    last, pat_spec, carry = lax.optimization_barrier((parts[1], pat_spec, carry))
    late = [last, send(last, core)]
    corr, smooth = match(orientation, pat_spec, table, inverse, late, [held[1], crossed[1]], carry, count, groups)
    return corr.T, smooth.T


def solution(mesh):
    placed = (P(("grp", "scan"), None, None), P("scan", None, None), P(), P(), P())
    return jax.shard_map(
        on_device,
        mesh=mesh,
        in_specs=placed,
        out_specs=(P(("grp", "scan"), None), P(("grp", "scan"), None)),
        check_vma=False,
    )
```

```python
import functools
import math

import jax
import jax.numpy as jnp
import numpy as np
from jax import lax
from jax.experimental import pallas as pl
from jax.experimental.pallas import tpu as pltpu
from jax.sharding import PartitionSpec as P

RADII = 64
ANGLES = 256
HALF = ANGLES // 2
GAINS = 8
TMPL_PER_GROUP = 2
LANES = 128
BLOCK = 16
ROWS = 16
PER_DEVICE = 2
F32 = jnp.float32
BF16 = jnp.bfloat16
CONTRACT_LAST = (((1,), (1,)), ((), ()))


def make_tables():
    along = np.arange(ANGLES, dtype=np.int32)
    modes = np.arange(HALF + 1, dtype=np.int32)
    scale = np.float32(2.0 * math.pi / ANGLES)
    phase = scale * (along[:, None] * modes[None, :] % ANGLES).astype(np.float32)
    cos, sin = np.cos(phase), np.sin(phase)
    basis = np.concatenate([cos, sin[:, 1:HALF]], axis=1)
    norm = np.float32(1.0 / (ANGLES * math.sqrt(RADII * ANGLES)))
    weight = np.where((modes == 0) | (modes == HALF), 1.0, 2.0).astype(np.float32)
    inv_cos = weight[None, :] * cos * norm
    inv_sin = -weight[None, :] * sin * norm
    inverse = np.concatenate([inv_cos, inv_sin[:, 1:HALF]], axis=1)
    return basis.T.astype(jnp.bfloat16), inverse.astype(jnp.bfloat16)


PITCH = LANES + 8
SIDE = 2 * BLOCK + 8


def arrange_kernel(pat_hbm, tmpl_hbm, table_hbm, out_ref, own_ref, table_ref, pat_ref, raw_ref, sem, side_sem):
    chunks = pat_ref.shape[0] // ROWS

    def fetch(c):
        part = pl.ds(c * ROWS, ROWS)
        return pltpu.make_async_copy(pat_hbm.at[part], pat_ref.at[part], sem.at[c])

    sides = [
        pltpu.make_async_copy(tmpl_hbm, own_ref, side_sem.at[0]),
        pltpu.make_async_copy(table_hbm, table_ref, side_sem.at[1]),
    ]
    for c in range(chunks):
        fetch(c).start()
    for copy in sides:
        copy.start()
    for c in range(chunks):
        fetch(c).wait()
        for p in range(ROWS):
            wide = pat_ref[c * ROWS + p].astype(F32)
            raw_ref[c % 2, 0, pl.ds(p, RADII, stride=ROWS + 8), :] = wide[:, :LANES]
            raw_ref[c % 2, 1, pl.ds(p, RADII, stride=ROWS + 8), :] = wide[:, LANES:]
        for r in range(RADII):
            at = pl.ds(r * (ROWS + 8), ROWS)
            out_ref[r, pl.ds(c * ROWS, ROWS), :] = jnp.concatenate(
                [raw_ref[c % 2, 0, at, :], raw_ref[c % 2, 1, at, :]], axis=1
            ).astype(BF16)
    for copy in sides:
        copy.wait()


def pattern_kernel(bin_ref, gain_ref, rows_ref, inner_ref, outer_ref, table_ref, out_ref, edge_ref, weight_ref, spec_ref):
    count = rows_ref.shape[1]
    spare = LANES - count
    pitch = spare + 8
    even = lax.axis_index("scan") % 2 == 0
    edge_ref[...] = jnp.zeros(edge_ref.shape, F32)
    inner, outer = inner_ref[0].astype(F32), outer_ref[0].astype(F32)
    for at, wide in ((0, jnp.where(even, inner, outer)), (spare - 1, jnp.where(even, outer, inner))):
        edge_ref[0, pl.ds(at, RADII, stride=pitch), :] = wide[:, :LANES]
        edge_ref[1, pl.ds(at, RADII, stride=pitch), :] = wide[:, LANES:]
    for r in range(RADII):
        weight_ref[pl.ds(r, 1), :] = jnp.full((1, LANES), gain_ref[bin_ref[r]], F32)
    for r in range(0, RADII, 2):
        rows = []
        for u in (r, r + 1):
            at = pl.ds(u * pitch, spare)
            rows += [rows_ref[u], jnp.concatenate([edge_ref[0, at, :], edge_ref[1, at, :]], axis=1).astype(BF16)]
        spec = lax.dot_general(
            table_ref[...], jnp.concatenate(rows, axis=0), CONTRACT_LAST, preferred_element_type=F32
        )
        for u in (r, r + 1):
            one = spec[:, (u - r) * LANES : (u - r + 1) * LANES] * weight_ref[pl.ds(u, 1), :]
            spec_ref[pl.ds(u, HALF, stride=PITCH), :] = one[:HALF]
            spec_ref[pl.ds(RADII + u, HALF, stride=PITCH), :] = one[HALF:]
    for k in range(HALF):
        out_ref[k] = spec_ref[pl.ds(k * PITCH, LANES), :].astype(BF16)


def match_kernel(pat_ref, table_ref, inv_ref, *refs, held, final):
    parts, refs = refs[: len(held)], refs[len(held) :]
    if final:
        orient_ref, rows_in, corr_ref, smooth_ref, side_ref, cross_ref, rows_ref = refs
        rows_ref[...] = rows_in[...]
    else:
        rows_ref, side_ref, cross_ref = refs
    index = lax.axis_index("scan")
    blocks = [(part, i, mask) for part, masks in zip(parts, held) for i, mask in enumerate(masks)]
    low = lax.broadcasted_iota(jnp.int32, (HALF, LANES), 1) < RADII
    low_edge = lax.broadcasted_iota(jnp.int32, (BLOCK, LANES), 1) < RADII
    for begin in range(0, len(blocks), BLOCK // PER_DEVICE):
        chunk = blocks[begin : begin + BLOCK // PER_DEVICE]
        for number in range(0, len(chunk), 2):
            (part, i, _), (other, j, _) = chunk[number : number + 2]
            raw = jnp.concatenate([part[pl.ds(i * PER_DEVICE, PER_DEVICE)], other[pl.ds(j * PER_DEVICE, PER_DEVICE)]])
            raw = raw.reshape(2 * PER_DEVICE * RADII, ANGLES)
            both = lax.dot_general(table_ref[...], raw, CONTRACT_LAST, preferred_element_type=F32)
            for u in (0, 1):
                t = (number + u) * PER_DEVICE
                spec = both[:, u * LANES : (u + 1) * LANES]
                cos, sin = spec[:HALF], spec[HALF:]
                turned_cos, turned_sin = pltpu.roll(cos, RADII, 1), pltpu.roll(sin, RADII, 1)
                side_ref[pl.ds(t, HALF, stride=SIDE), :] = jnp.where(low, cos, turned_sin)
                side_ref[pl.ds(t + 1, HALF, stride=SIDE), :] = jnp.where(low, turned_cos, sin)
                side_ref[pl.ds(BLOCK + t, HALF, stride=SIDE), :] = jnp.where(low, sin, -turned_cos)
                side_ref[pl.ds(BLOCK + t + 1, HALF, stride=SIDE), :] = jnp.where(low, turned_sin, -cos)
        none = jnp.zeros((2 * BLOCK, LANES), BF16)
        for k in range(0, HALF, 2):
            left = [side_ref[pl.ds(u * SIDE, 2 * BLOCK), :] for u in (k, k + 1)]
            if k == 0:
                edge = left[0][:BLOCK]
                left[0] = jnp.concatenate([jnp.where(low_edge, edge, 0.0), jnp.where(low_edge, 0.0, edge)], axis=0)
            left = [jnp.concatenate([left[0].astype(BF16), none], axis=1), jnp.concatenate([none, left[1].astype(BF16)], axis=1)]
            right = pat_ref[pl.ds(k, 2)].reshape(2 * LANES, LANES)
            both = jnp.dot(jnp.concatenate(left, axis=0), right, preferred_element_type=F32)
            cross_ref[pl.ds(k * SIDE, 2 * BLOCK), :] = both[: 2 * BLOCK]
            cross_ref[pl.ds((k + 1) * SIDE, 2 * BLOCK), :] = both[2 * BLOCK :]
        rows = []
        for t in range(0, len(chunk) * PER_DEVICE, 2):
            cross = [
                jnp.concatenate(
                    [cross_ref[pl.ds(u, HALF, stride=SIDE), :], cross_ref[pl.ds(BLOCK + u, HALF, stride=SIDE), :]], axis=0
                ).astype(BF16)
                for u in (t, t + 1)
            ]
            shifted = jnp.dot(inv_ref[...], jnp.concatenate(cross, axis=1), preferred_element_type=F32)
            top = jnp.max(shifted, axis=0, keepdims=True)
            rows += [top[:, :LANES], top[:, LANES:]]
        for number, (_, _, mask) in enumerate(chunk):
            for e in range(PER_DEVICE):
                where = (index ^ mask) * PER_DEVICE + e
                rows_ref[pl.ds(where, 1), :] = rows[number * PER_DEVICE + e]
    if not final:
        return
    corr = rows_ref[...]
    corr_ref[...] = corr[:, : corr_ref.shape[1]]
    total = corr.shape[0]
    groups = orient_ref[...].astype(F32)
    if total % LANES:
        groups = jnp.concatenate([groups, jnp.zeros((1, LANES - total % LANES), F32)], axis=1)
    groups = jnp.broadcast_to(groups, (LANES, groups.shape[1])).T[:total]
    best = [
        jnp.max(jnp.where(groups == float(g), corr, -jnp.inf), axis=0, keepdims=True) for g in range(smooth_ref.shape[0])
    ]
    best = jnp.concatenate(best, axis=0)
    smooth = 0.25 * (pltpu.roll(best, 1, 1) + 2.0 * best + pltpu.roll(best, LANES - 1, 1))
    smooth_ref[...] = smooth[:, : smooth_ref.shape[1]]


VMEM = pl.BlockSpec(memory_space=pltpu.VMEM)
SMEM = pl.BlockSpec(memory_space=pltpu.SMEM)
HBM = pl.BlockSpec(memory_space=pltpu.HBM)


def arrange(patterns, templates, table):
    count = patterns.shape[0]
    args = (patterns, templates, table)
    return pl.pallas_call(
        arrange_kernel,
        out_shape=(
            jax.ShapeDtypeStruct((RADII, count, ANGLES), BF16),
            jax.ShapeDtypeStruct(templates.shape, BF16),
            jax.ShapeDtypeStruct(table.shape, BF16),
        ),
        in_specs=[HBM] * 3,
        out_specs=(VMEM,) * 3,
        scratch_shapes=[
            pltpu.VMEM(patterns.shape, BF16),
            pltpu.VMEM((2, 2, RADII * (ROWS + 8), LANES), F32),
            pltpu.SemaphoreType.DMA((count // ROWS,)),
            pltpu.SemaphoreType.DMA((2,)),
        ],
        compiler_params=pltpu.CompilerParams(vmem_limit_bytes=16 << 20),
        name="arrange",
    )(*(pltpu.with_memory_space_constraint(x, pltpu.HBM) for x in args))


def pattern_spectra(bins, gains, rows, inner, outer, table):
    spare = LANES - rows.shape[1]
    return pl.pallas_call(
        pattern_kernel,
        out_shape=jax.ShapeDtypeStruct((HALF, LANES, LANES), BF16),
        in_specs=[SMEM] * 2 + [VMEM] * 4,
        out_specs=VMEM,
        scratch_shapes=[
            pltpu.VMEM((2, RADII * (spare + 8), LANES), F32),
            pltpu.VMEM((RADII, LANES), F32),
            pltpu.VMEM((HALF * PITCH, LANES), F32),
        ],
        compiler_params=pltpu.CompilerParams(vmem_limit_bytes=16 << 20),
        name="pattern_spectra",
    )(bins, gains, rows, inner, outer, table)


def match(pat_spec, table, inverse, parts, held, orientation, carry, count, groups):
    total = orientation.shape[1]
    rows = jax.ShapeDtypeStruct((total, LANES), F32)
    outs = [jax.ShapeDtypeStruct((total, count), F32), jax.ShapeDtypeStruct((groups, count), F32)] if carry else [rows]
    scratch = [pltpu.VMEM((HALF * SIDE, LANES), F32), pltpu.VMEM((HALF * SIDE, LANES), F32)]
    more = [orientation, *carry] if carry else []
    return pl.pallas_call(
        functools.partial(match_kernel, held=held, final=bool(carry)),
        out_shape=outs,
        in_specs=[VMEM] * (3 + len(parts) + len(more)),
        out_specs=[VMEM] * len(outs),
        scratch_shapes=scratch + [pltpu.VMEM(rows.shape, F32)] * bool(carry),
        compiler_params=pltpu.CompilerParams(vmem_limit_bytes=16 << 20),
        name="match",
    )(pat_spec, table, inverse, *parts, *more)


def on_device(patterns, templates, radius_bin, radial_gain, orientation):
    table, inverse = make_tables()
    table, inverse = jnp.asarray(table), jnp.asarray(inverse)
    count = patterns.shape[0]
    size = lax.axis_size("scan")
    groups = templates.shape[0] * size // TMPL_PER_GROUP
    orientation = orientation.reshape(1, -1)
    bits = [1 << b for b in reversed(range(size.bit_length() - 1))]
    far, near, middle, core = bits[0], bits[1], bits[2:-1], bits[-1]

    def send(part, mask):
        return lax.ppermute(part, "scan", [(i, i ^ mask) for i in range(size)])

    masks = [0, far, far ^ near, near]
    came = [send(templates, mask) for mask in masks[1:]]
    even = lax.axis_index("scan") % 2 == 0
    leading, last = patterns[:1], patterns[count - 1 :]
    inner, outer = jnp.where(even, last, leading), jnp.where(even, leading, last)
    pairs = [(i, i + 1) for i in range(1, size - 1, 2)]
    inner = send(inner, 1)
    outer = lax.ppermute(outer, "scan", pairs + [(j, i) for i, j in pairs])
    rows, own, table = arrange(patterns, templates, table)
    came, rows, own, table, inner, outer = lax.optimization_barrier((came, rows, own, table, inner, outer))
    part = lax.optimization_barrier(jnp.concatenate([own] + came, axis=0))
    parts, held = [part], [masks]
    for mask in middle:
        if mask != middle[0]:
            parts, held = [jnp.concatenate(parts, axis=0)], [held[0] + held[1]]
        parts, held = parts + [send(parts[0], mask)], held + [[m ^ mask for m in held[0]]]
    pat_spec = pattern_spectra(radius_bin, radial_gain, rows, inner, outer, table)
    crossed = [[m ^ core for m in masks] for masks in held]
    early = [parts[0], send(parts[0], core)]
    carry = match(pat_spec, table, inverse, early, [held[0], crossed[0]], orientation, [], count, groups)
    last, pat_spec, carry = lax.optimization_barrier((parts[1], pat_spec, carry))
    late = [last, send(last, core)]
    corr, smooth = match(pat_spec, table, inverse, late, [held[1], crossed[1]], orientation, carry, count, groups)
    return corr.T, smooth.T


def solution(mesh):
    placed = (P(("grp", "scan"), None, None), P("scan", None, None), P(), P(), P())
    return jax.shard_map(
        on_device,
        mesh=mesh,
        in_specs=placed,
        out_specs=(P(("grp", "scan"), None), P(("grp", "scan"), None)),
        check_vma=False,
    )
```

```python
import functools
import math

import jax
import jax.numpy as jnp
import numpy as np
from jax import lax
from jax.experimental import pallas as pl
from jax.experimental.pallas import tpu as pltpu
from jax.sharding import PartitionSpec as P

RADII = 64
ANGLES = 256
HALF = ANGLES // 2
GAINS = 8
TMPL_PER_GROUP = 2
LANES = 128
BLOCK = 16
ROWS = 16
PER_DEVICE = 2
F32 = jnp.float32
BF16 = jnp.bfloat16
CONTRACT_LAST = (((1,), (1,)), ((), ()))


def make_tables():
    along = np.arange(ANGLES, dtype=np.int32)
    modes = np.arange(HALF + 1, dtype=np.int32)
    scale = np.float32(2.0 * math.pi / ANGLES)
    phase = scale * (along[:, None] * modes[None, :] % ANGLES).astype(np.float32)
    cos, sin = np.cos(phase), np.sin(phase)
    basis = np.concatenate([cos, sin[:, 1:HALF]], axis=1)
    norm = np.float32(1.0 / (ANGLES * math.sqrt(RADII * ANGLES)))
    weight = np.where((modes == 0) | (modes == HALF), 1.0, 2.0).astype(np.float32)
    inv_cos = weight[None, :] * cos * norm
    inv_sin = -weight[None, :] * sin * norm
    inverse = np.concatenate([inv_cos, inv_sin[:, 1:HALF]], axis=1)
    return basis.T.astype(jnp.bfloat16), inverse.astype(jnp.bfloat16)


PITCH = LANES + 8


def arrange_kernel(pat_hbm, tmpl_hbm, table_hbm, out_ref, own_ref, table_ref, pat_ref, raw_ref, sem, side_sem):
    chunks = pat_ref.shape[0] // ROWS

    def fetch(c):
        part = pl.ds(c * ROWS, ROWS)
        return pltpu.make_async_copy(pat_hbm.at[part], pat_ref.at[part], sem.at[c])

    sides = [
        pltpu.make_async_copy(tmpl_hbm, own_ref, side_sem.at[0]),
        pltpu.make_async_copy(table_hbm, table_ref, side_sem.at[1]),
    ]
    for c in range(chunks):
        fetch(c).start()
    for copy in sides:
        copy.start()
    for c in range(chunks):
        fetch(c).wait()
        for p in range(ROWS):
            wide = pat_ref[c * ROWS + p].astype(F32)
            raw_ref[c % 2, 0, pl.ds(p, RADII, stride=ROWS + 8), :] = wide[:, :LANES]
            raw_ref[c % 2, 1, pl.ds(p, RADII, stride=ROWS + 8), :] = wide[:, LANES:]
        for r in range(RADII):
            at = pl.ds(r * (ROWS + 8), ROWS)
            out_ref[r, pl.ds(c * ROWS, ROWS), :] = jnp.concatenate(
                [raw_ref[c % 2, 0, at, :], raw_ref[c % 2, 1, at, :]], axis=1
            ).astype(BF16)
    for copy in sides:
        copy.wait()


def pattern_kernel(bin_ref, gain_ref, rows_ref, inner_ref, outer_ref, table_ref, out_ref, edge_ref, weight_ref, spec_ref):
    count = rows_ref.shape[1]
    spare = LANES - count
    pitch = spare + 8
    even = lax.axis_index("scan") % 2 == 0
    edge_ref[...] = jnp.zeros(edge_ref.shape, F32)
    inner, outer = inner_ref[0].astype(F32), outer_ref[0].astype(F32)
    for at, wide in ((0, jnp.where(even, inner, outer)), (spare - 1, jnp.where(even, outer, inner))):
        edge_ref[0, pl.ds(at, RADII, stride=pitch), :] = wide[:, :LANES]
        edge_ref[1, pl.ds(at, RADII, stride=pitch), :] = wide[:, LANES:]
    for r in range(RADII):
        weight_ref[pl.ds(r, 1), :] = jnp.full((1, LANES), gain_ref[bin_ref[r]], F32)
    for r in range(0, RADII, 2):
        rows = []
        for u in (r, r + 1):
            at = pl.ds(u * pitch, spare)
            rows += [rows_ref[u], jnp.concatenate([edge_ref[0, at, :], edge_ref[1, at, :]], axis=1).astype(BF16)]
        spec = lax.dot_general(
            table_ref[...], jnp.concatenate(rows, axis=0), CONTRACT_LAST, preferred_element_type=F32
        )
        for u in (r, r + 1):
            one = spec[:, (u - r) * LANES : (u - r + 1) * LANES] * weight_ref[pl.ds(u, 1), :]
            spec_ref[pl.ds(u, HALF, stride=PITCH), :] = one[:HALF]
            spec_ref[pl.ds(RADII + u, HALF, stride=PITCH), :] = one[HALF:]
    for k in range(HALF):
        out_ref[k] = spec_ref[pl.ds(k * PITCH, LANES), :].astype(BF16)


def match_kernel(pat_ref, table_ref, inv_ref, *refs, held, block, first, final):
    side = 2 * block + 8
    parts, refs = refs[: len(held)], refs[len(held) :]
    if final:
        orient_ref, rows_in, corr_ref, smooth_ref, side_ref, cross_ref, rows_ref = refs
    elif first:
        rows_ref, side_ref, cross_ref = refs
    else:
        rows_in, rows_ref, side_ref, cross_ref = refs
    if not first:
        rows_ref[...] = rows_in[...]
    index = lax.axis_index("scan")
    blocks = [(part, i, mask) for part, masks in zip(parts, held) for i, mask in enumerate(masks)]
    low = lax.broadcasted_iota(jnp.int32, (HALF, LANES), 1) < RADII
    low_edge = lax.broadcasted_iota(jnp.int32, (block, LANES), 1) < RADII
    for begin in range(0, len(blocks), block // PER_DEVICE):
        chunk = blocks[begin : begin + block // PER_DEVICE]
        for number in range(0, len(chunk), 2):
            (part, i, _), (other, j, _) = chunk[number : number + 2]
            raw = jnp.concatenate([part[pl.ds(i * PER_DEVICE, PER_DEVICE)], other[pl.ds(j * PER_DEVICE, PER_DEVICE)]])
            raw = raw.reshape(2 * PER_DEVICE * RADII, ANGLES)
            both = lax.dot_general(table_ref[...], raw, CONTRACT_LAST, preferred_element_type=F32)
            for u in (0, 1):
                t = (number + u) * PER_DEVICE
                spec = both[:, u * LANES : (u + 1) * LANES]
                cos, sin = spec[:HALF], spec[HALF:]
                turned_cos, turned_sin = pltpu.roll(cos, RADII, 1), pltpu.roll(sin, RADII, 1)
                side_ref[pl.ds(t, HALF, stride=side), :] = jnp.where(low, cos, turned_sin)
                side_ref[pl.ds(t + 1, HALF, stride=side), :] = jnp.where(low, turned_cos, sin)
                side_ref[pl.ds(block + t, HALF, stride=side), :] = jnp.where(low, sin, -turned_cos)
                side_ref[pl.ds(block + t + 1, HALF, stride=side), :] = jnp.where(low, turned_sin, -cos)
        none = jnp.zeros((2 * block, LANES), BF16)
        for k in range(0, HALF, 2):
            left = [side_ref[pl.ds(u * side, 2 * block), :] for u in (k, k + 1)]
            if k == 0:
                edge = left[0][:block]
                left[0] = jnp.concatenate([jnp.where(low_edge, edge, 0.0), jnp.where(low_edge, 0.0, edge)], axis=0)
            left = [jnp.concatenate([left[0].astype(BF16), none], axis=1), jnp.concatenate([none, left[1].astype(BF16)], axis=1)]
            right = pat_ref[pl.ds(k, 2)].reshape(2 * LANES, LANES)
            both = jnp.dot(jnp.concatenate(left, axis=0), right, preferred_element_type=F32)
            cross_ref[pl.ds(k * side, 2 * block), :] = both[: 2 * block]
            cross_ref[pl.ds((k + 1) * side, 2 * block), :] = both[2 * block :]
        rows = []
        for t in range(0, len(chunk) * PER_DEVICE, 2):
            cross = [
                jnp.concatenate(
                    [cross_ref[pl.ds(u, HALF, stride=side), :], cross_ref[pl.ds(block + u, HALF, stride=side), :]], axis=0
                ).astype(BF16)
                for u in (t, t + 1)
            ]
            shifted = jnp.dot(inv_ref[...], jnp.concatenate(cross, axis=1), preferred_element_type=F32)
            top = jnp.max(shifted, axis=0, keepdims=True)
            rows += [top[:, :LANES], top[:, LANES:]]
        for number, (_, _, mask) in enumerate(chunk):
            for e in range(PER_DEVICE):
                where = (index ^ mask) * PER_DEVICE + e
                rows_ref[pl.ds(where, 1), :] = rows[number * PER_DEVICE + e]
    if not final:
        return
    corr = rows_ref[...]
    corr_ref[...] = corr[:, : corr_ref.shape[1]]
    total = corr.shape[0]
    groups = orient_ref[...].astype(F32)
    if total % LANES:
        groups = jnp.concatenate([groups, jnp.zeros((1, LANES - total % LANES), F32)], axis=1)
    groups = jnp.broadcast_to(groups, (LANES, groups.shape[1])).T[:total]
    best = [
        jnp.max(jnp.where(groups == float(g), corr, -jnp.inf), axis=0, keepdims=True) for g in range(smooth_ref.shape[0])
    ]
    best = jnp.concatenate(best, axis=0)
    smooth = 0.25 * (pltpu.roll(best, 1, 1) + 2.0 * best + pltpu.roll(best, LANES - 1, 1))
    smooth_ref[...] = smooth[:, : smooth_ref.shape[1]]


VMEM = pl.BlockSpec(memory_space=pltpu.VMEM)
SMEM = pl.BlockSpec(memory_space=pltpu.SMEM)
HBM = pl.BlockSpec(memory_space=pltpu.HBM)


def arrange(patterns, templates, table):
    count = patterns.shape[0]
    args = (patterns, templates, table)
    return pl.pallas_call(
        arrange_kernel,
        out_shape=(
            jax.ShapeDtypeStruct((RADII, count, ANGLES), BF16),
            jax.ShapeDtypeStruct(templates.shape, BF16),
            jax.ShapeDtypeStruct(table.shape, BF16),
        ),
        in_specs=[HBM] * 3,
        out_specs=(VMEM,) * 3,
        scratch_shapes=[
            pltpu.VMEM(patterns.shape, BF16),
            pltpu.VMEM((2, 2, RADII * (ROWS + 8), LANES), F32),
            pltpu.SemaphoreType.DMA((count // ROWS,)),
            pltpu.SemaphoreType.DMA((2,)),
        ],
        compiler_params=pltpu.CompilerParams(vmem_limit_bytes=16 << 20),
        name="arrange",
    )(*(pltpu.with_memory_space_constraint(x, pltpu.HBM) for x in args))


def pattern_spectra(bins, gains, rows, inner, outer, table):
    spare = LANES - rows.shape[1]
    return pl.pallas_call(
        pattern_kernel,
        out_shape=jax.ShapeDtypeStruct((HALF, LANES, LANES), BF16),
        in_specs=[SMEM] * 2 + [VMEM] * 4,
        out_specs=VMEM,
        scratch_shapes=[
            pltpu.VMEM((2, RADII * (spare + 8), LANES), F32),
            pltpu.VMEM((RADII, LANES), F32),
            pltpu.VMEM((HALF * PITCH, LANES), F32),
        ],
        compiler_params=pltpu.CompilerParams(vmem_limit_bytes=16 << 20),
        name="pattern_spectra",
    )(bins, gains, rows, inner, outer, table)


def match(pat_spec, table, inverse, parts, held, carry, total, final=None):
    block = min(BLOCK, sum(part.shape[0] for part in parts))
    rows = jax.ShapeDtypeStruct((total, LANES), F32)
    outs = [rows]
    if final:
        orientation, *outs = final
        carry = [orientation, *carry]
    scratch = [pltpu.VMEM((HALF * (2 * block + 8), LANES), F32)] * 2
    return pl.pallas_call(
        functools.partial(match_kernel, held=held, block=block, first=not carry, final=bool(final)),
        out_shape=outs,
        in_specs=[VMEM] * (3 + len(parts) + len(carry)),
        out_specs=[VMEM] * len(outs),
        scratch_shapes=scratch + [pltpu.VMEM(rows.shape, F32)] * bool(final),
        compiler_params=pltpu.CompilerParams(vmem_limit_bytes=16 << 20),
        name="match",
    )(pat_spec, table, inverse, *parts, *carry)


def on_device(patterns, templates, radius_bin, radial_gain, orientation):
    table, inverse = make_tables()
    table, inverse = jnp.asarray(table), jnp.asarray(inverse)
    count = patterns.shape[0]
    size = lax.axis_size("scan")
    groups = templates.shape[0] * size // TMPL_PER_GROUP
    orientation = orientation.reshape(1, -1)
    bits = [1 << b for b in reversed(range(size.bit_length() - 1))]
    far, near, middle, core = bits[0], bits[1], bits[2:-1], bits[-1]

    def send(part, mask):
        return lax.ppermute(part, "scan", [(i, i ^ mask) for i in range(size)])

    masks = [0, far, far ^ near, near]
    came = [send(templates, mask) for mask in masks[1:]]
    even = lax.axis_index("scan") % 2 == 0
    leading, last = patterns[:1], patterns[count - 1 :]
    inner, outer = jnp.where(even, last, leading), jnp.where(even, leading, last)
    pairs = [(i, i + 1) for i in range(1, size - 1, 2)]
    inner = send(inner, 1)
    outer = lax.ppermute(outer, "scan", pairs + [(j, i) for i, j in pairs])
    rows, own, table = arrange(patterns, templates, table)
    came, rows, own, table, inner, outer = lax.optimization_barrier((came, rows, own, table, inner, outer))
    part = lax.optimization_barrier(jnp.concatenate([own] + came, axis=0))
    parts, held = [part], [masks]
    for mask in middle:
        if mask != middle[0]:
            parts, held = [jnp.concatenate(parts, axis=0)], [held[0] + held[1]]
        parts, held = parts + [send(parts[0], mask)], held + [[m ^ mask for m in held[0]]]
    pat_spec = pattern_spectra(radius_bin, radial_gain, rows, inner, outer, table)
    crossed = [[m ^ core for m in masks] for masks in held]
    early = [parts[0], send(parts[0], core)]
    total = orientation.shape[1]
    outs = jax.ShapeDtypeStruct((total, count), F32), jax.ShapeDtypeStruct((groups, count), F32)
    carry = match(pat_spec, table, inverse, early, [held[0], crossed[0]], [], total)
    last, pat_spec, carry = lax.optimization_barrier((parts[1], pat_spec, carry))
    over = send(last, core)
    carry = match(pat_spec, table, inverse, [last], [held[1]], carry, total)
    over, carry = lax.optimization_barrier((over, carry))
    corr, smooth = match(pat_spec, table, inverse, [over], [crossed[1]], carry, total, (orientation, *outs))
    return corr.T, smooth.T


def solution(mesh):
    placed = (P(("grp", "scan"), None, None), P("scan", None, None), P(), P(), P())
    return jax.shard_map(
        on_device,
        mesh=mesh,
        in_specs=placed,
        out_specs=(P(("grp", "scan"), None), P(("grp", "scan"), None)),
        check_vma=False,
    )
```

```python
import functools
import math

import jax
import jax.numpy as jnp
import numpy as np
from jax import lax
from jax.experimental import pallas as pl
from jax.experimental.pallas import tpu as pltpu
from jax.sharding import PartitionSpec as P

RADII = 64
ANGLES = 256
HALF = ANGLES // 2
GAINS = 8
TMPL_PER_GROUP = 2
LANES = 128
BLOCK = 16
ROWS = 16
PER_DEVICE = 2
F32 = jnp.float32
BF16 = jnp.bfloat16
CONTRACT_LAST = (((1,), (1,)), ((), ()))


def make_tables():
    along = np.arange(ANGLES, dtype=np.int32)
    modes = np.arange(HALF + 1, dtype=np.int32)
    scale = np.float32(2.0 * math.pi / ANGLES)
    phase = scale * (along[:, None] * modes[None, :] % ANGLES).astype(np.float32)
    cos, sin = np.cos(phase), np.sin(phase)
    basis = np.concatenate([cos, sin[:, 1:HALF]], axis=1)
    norm = np.float32(1.0 / (ANGLES * math.sqrt(RADII * ANGLES)))
    weight = np.where((modes == 0) | (modes == HALF), 1.0, 2.0).astype(np.float32)
    inv_cos = weight[None, :] * cos * norm
    inv_sin = -weight[None, :] * sin * norm
    inverse = np.concatenate([inv_cos, inv_sin[:, 1:HALF]], axis=1)
    return basis.T.astype(jnp.bfloat16), inverse.astype(jnp.bfloat16)


PITCH = LANES + 8


def arrange_kernel(pat_hbm, tmpl_hbm, table_hbm, out_ref, own_ref, table_ref, tail_ref, pat_ref, raw_ref, sem, side_sem):
    chunks = pat_ref.shape[0] // ROWS

    def fetch(c):
        part = pl.ds(c * ROWS, ROWS)
        return pltpu.make_async_copy(pat_hbm.at[part], pat_ref.at[part], sem.at[c])

    sides = [
        pltpu.make_async_copy(tmpl_hbm, own_ref, side_sem.at[0]),
        pltpu.make_async_copy(table_hbm, table_ref, side_sem.at[1]),
        pltpu.make_async_copy(pat_hbm.at[pl.ds(pat_ref.shape[0], tail_ref.shape[0])], tail_ref, side_sem.at[2]),
    ]
    for c in range(chunks):
        fetch(c).start()
    for copy in sides:
        copy.start()
    for c in range(chunks):
        fetch(c).wait()
        for p in range(ROWS):
            wide = pat_ref[c * ROWS + p].astype(F32)
            raw_ref[c % 2, 0, pl.ds(p, RADII, stride=ROWS + 8), :] = wide[:, :LANES]
            raw_ref[c % 2, 1, pl.ds(p, RADII, stride=ROWS + 8), :] = wide[:, LANES:]
        for r in range(RADII):
            at = pl.ds(r * (ROWS + 8), ROWS)
            out_ref[r, pl.ds(c * ROWS, ROWS), :] = jnp.concatenate(
                [raw_ref[c % 2, 0, at, :], raw_ref[c % 2, 1, at, :]], axis=1
            ).astype(BF16)
    for copy in sides:
        copy.wait()


def pattern_kernel(bin_ref, gain_ref, rows_ref, tail_ref, inner_ref, outer_ref, table_ref, out_ref, edge_ref, weight_ref, spec_ref):
    spare = LANES - rows_ref.shape[1]
    tail = tail_ref.shape[0]
    pitch = spare + 8
    even = lax.axis_index("scan") % 2 == 0
    zero = jnp.zeros((spare - tail, LANES), F32)
    for r in range(RADII):
        edge_ref[0, pl.ds(r * pitch + tail, spare - tail), :] = zero
        edge_ref[1, pl.ds(r * pitch + tail, spare - tail), :] = zero

    def put(at, wide):
        edge_ref[0, pl.ds(at, RADII, stride=pitch), :] = wide[:, :LANES]
        edge_ref[1, pl.ds(at, RADII, stride=pitch), :] = wide[:, LANES:]

    for p in range(tail):
        put(p, tail_ref[p].astype(F32))
    inner, outer = inner_ref[0].astype(F32), outer_ref[0].astype(F32)
    put(tail, jnp.where(even, inner, outer))
    put(spare - 1, jnp.where(even, outer, inner))
    for r in range(RADII):
        weight_ref[pl.ds(r, 1), :] = jnp.full((1, LANES), gain_ref[bin_ref[r]], F32)
    for r in range(0, RADII, 2):
        rows = []
        for u in (r, r + 1):
            at = pl.ds(u * pitch, spare)
            rows += [rows_ref[u], jnp.concatenate([edge_ref[0, at, :], edge_ref[1, at, :]], axis=1).astype(BF16)]
        spec = lax.dot_general(
            table_ref[...], jnp.concatenate(rows, axis=0), CONTRACT_LAST, preferred_element_type=F32
        )
        for u in (r, r + 1):
            one = spec[:, (u - r) * LANES : (u - r + 1) * LANES] * weight_ref[pl.ds(u, 1), :]
            spec_ref[pl.ds(u, HALF, stride=PITCH), :] = one[:HALF]
            spec_ref[pl.ds(RADII + u, HALF, stride=PITCH), :] = one[HALF:]
    for k in range(HALF):
        out_ref[k] = spec_ref[pl.ds(k * PITCH, LANES), :].astype(BF16)


def match_kernel(pat_ref, table_ref, inv_ref, *refs, held, block, first, final):
    side = 2 * block + 8
    parts, refs = refs[: len(held)], refs[len(held) :]
    if final:
        orient_ref, rows_in, corr_ref, smooth_ref, side_ref, cross_ref, rows_ref = refs
    elif first:
        rows_ref, side_ref, cross_ref = refs
    else:
        rows_in, rows_ref, side_ref, cross_ref = refs
    if not first:
        rows_ref[...] = rows_in[...]
    index = lax.axis_index("scan")
    blocks = [(part, i, mask) for part, masks in zip(parts, held) for i, mask in enumerate(masks)]
    low = lax.broadcasted_iota(jnp.int32, (HALF, LANES), 1) < RADII
    low_edge = lax.broadcasted_iota(jnp.int32, (block, LANES), 1) < RADII
    for begin in range(0, len(blocks), block // PER_DEVICE):
        chunk = blocks[begin : begin + block // PER_DEVICE]
        for number in range(0, len(chunk), 2):
            (part, i, _), (other, j, _) = chunk[number : number + 2]
            raw = jnp.concatenate([part[pl.ds(i * PER_DEVICE, PER_DEVICE)], other[pl.ds(j * PER_DEVICE, PER_DEVICE)]])
            raw = raw.reshape(2 * PER_DEVICE * RADII, ANGLES)
            both = lax.dot_general(table_ref[...], raw, CONTRACT_LAST, preferred_element_type=F32)
            for u in (0, 1):
                t = (number + u) * PER_DEVICE
                spec = both[:, u * LANES : (u + 1) * LANES]
                cos, sin = spec[:HALF], spec[HALF:]
                turned_cos, turned_sin = pltpu.roll(cos, RADII, 1), pltpu.roll(sin, RADII, 1)
                side_ref[pl.ds(t, HALF, stride=side), :] = jnp.where(low, cos, turned_sin)
                side_ref[pl.ds(t + 1, HALF, stride=side), :] = jnp.where(low, turned_cos, sin)
                side_ref[pl.ds(block + t, HALF, stride=side), :] = jnp.where(low, sin, -turned_cos)
                side_ref[pl.ds(block + t + 1, HALF, stride=side), :] = jnp.where(low, turned_sin, -cos)
        none = jnp.zeros((2 * block, LANES), BF16)
        for k in range(0, HALF, 2):
            left = [side_ref[pl.ds(u * side, 2 * block), :] for u in (k, k + 1)]
            if k == 0:
                edge = left[0][:block]
                left[0] = jnp.concatenate([jnp.where(low_edge, edge, 0.0), jnp.where(low_edge, 0.0, edge)], axis=0)
            left = [jnp.concatenate([left[0].astype(BF16), none], axis=1), jnp.concatenate([none, left[1].astype(BF16)], axis=1)]
            right = pat_ref[pl.ds(k, 2)].reshape(2 * LANES, LANES)
            both = jnp.dot(jnp.concatenate(left, axis=0), right, preferred_element_type=F32)
            cross_ref[pl.ds(k * side, 2 * block), :] = both[: 2 * block]
            cross_ref[pl.ds((k + 1) * side, 2 * block), :] = both[2 * block :]
        rows = []
        for t in range(0, len(chunk) * PER_DEVICE, 2):
            cross = [
                jnp.concatenate(
                    [cross_ref[pl.ds(u, HALF, stride=side), :], cross_ref[pl.ds(block + u, HALF, stride=side), :]], axis=0
                ).astype(BF16)
                for u in (t, t + 1)
            ]
            shifted = jnp.dot(inv_ref[...], jnp.concatenate(cross, axis=1), preferred_element_type=F32)
            top = jnp.max(shifted, axis=0, keepdims=True)
            rows += [top[:, :LANES], top[:, LANES:]]
        for number, (_, _, mask) in enumerate(chunk):
            for e in range(PER_DEVICE):
                where = (index ^ mask) * PER_DEVICE + e
                rows_ref[pl.ds(where, 1), :] = rows[number * PER_DEVICE + e]
    if not final:
        return
    corr = rows_ref[...]
    corr_ref[...] = corr[:, : corr_ref.shape[1]]
    total = corr.shape[0]
    groups = orient_ref[...].astype(F32)
    if total % LANES:
        groups = jnp.concatenate([groups, jnp.zeros((1, LANES - total % LANES), F32)], axis=1)
    groups = jnp.broadcast_to(groups, (LANES, groups.shape[1])).T[:total]
    best = [
        jnp.max(jnp.where(groups == float(g), corr, -jnp.inf), axis=0, keepdims=True) for g in range(smooth_ref.shape[0])
    ]
    best = jnp.concatenate(best, axis=0)
    smooth = 0.25 * (pltpu.roll(best, 1, 1) + 2.0 * best + pltpu.roll(best, LANES - 1, 1))
    smooth_ref[...] = smooth[:, : smooth_ref.shape[1]]


VMEM = pl.BlockSpec(memory_space=pltpu.VMEM)
SMEM = pl.BlockSpec(memory_space=pltpu.SMEM)
HBM = pl.BlockSpec(memory_space=pltpu.HBM)


def arrange(patterns, templates, table):
    count = patterns.shape[0]
    head = count - count // (3 * ROWS) * ROWS
    args = (patterns, templates, table)
    return pl.pallas_call(
        arrange_kernel,
        out_shape=(
            jax.ShapeDtypeStruct((RADII, head, ANGLES), BF16),
            jax.ShapeDtypeStruct(templates.shape, BF16),
            jax.ShapeDtypeStruct(table.shape, BF16),
            jax.ShapeDtypeStruct((count - head,) + patterns.shape[1:], BF16),
        ),
        in_specs=[HBM] * 3,
        out_specs=(VMEM,) * 4,
        scratch_shapes=[
            pltpu.VMEM((head,) + patterns.shape[1:], BF16),
            pltpu.VMEM((2, 2, RADII * (ROWS + 8), LANES), F32),
            pltpu.SemaphoreType.DMA((head // ROWS,)),
            pltpu.SemaphoreType.DMA((3,)),
        ],
        compiler_params=pltpu.CompilerParams(vmem_limit_bytes=16 << 20),
        name="arrange",
    )(*(pltpu.with_memory_space_constraint(x, pltpu.HBM) for x in args))


def pattern_spectra(bins, gains, rows, tail, inner, outer, table):
    spare = LANES - rows.shape[1]
    return pl.pallas_call(
        pattern_kernel,
        out_shape=jax.ShapeDtypeStruct((HALF, LANES, LANES), BF16),
        in_specs=[SMEM] * 2 + [VMEM] * 5,
        out_specs=VMEM,
        scratch_shapes=[
            pltpu.VMEM((2, RADII * (spare + 8), LANES), F32),
            pltpu.VMEM((RADII, LANES), F32),
            pltpu.VMEM((HALF * PITCH, LANES), F32),
        ],
        compiler_params=pltpu.CompilerParams(vmem_limit_bytes=16 << 20),
        name="pattern_spectra",
    )(bins, gains, rows, tail, inner, outer, table)


def match(pat_spec, table, inverse, parts, held, carry, total, final=None):
    block = min(BLOCK, sum(part.shape[0] for part in parts))
    rows = jax.ShapeDtypeStruct((total, LANES), F32)
    outs = [rows]
    if final:
        orientation, *outs = final
        carry = [orientation, *carry]
    scratch = [pltpu.VMEM((HALF * (2 * block + 8), LANES), F32)] * 2
    return pl.pallas_call(
        functools.partial(match_kernel, held=held, block=block, first=not carry, final=bool(final)),
        out_shape=outs,
        in_specs=[VMEM] * (3 + len(parts) + len(carry)),
        out_specs=[VMEM] * len(outs),
        scratch_shapes=scratch + [pltpu.VMEM(rows.shape, F32)] * bool(final),
        compiler_params=pltpu.CompilerParams(vmem_limit_bytes=16 << 20),
        name="match",
    )(pat_spec, table, inverse, *parts, *carry)


def on_device(patterns, templates, radius_bin, radial_gain, orientation):
    table, inverse = make_tables()
    table, inverse = jnp.asarray(table), jnp.asarray(inverse)
    count = patterns.shape[0]
    size = lax.axis_size("scan")
    groups = templates.shape[0] * size // TMPL_PER_GROUP
    orientation = orientation.reshape(1, -1)
    bits = [1 << b for b in reversed(range(size.bit_length() - 1))]
    far, near, middle, core = bits[0], bits[1], bits[2:-1], bits[-1]

    def send(part, mask):
        return lax.ppermute(part, "scan", [(i, i ^ mask) for i in range(size)])

    masks = [0, far, far ^ near, near]
    came = [send(templates, mask) for mask in masks[1:]]
    even = lax.axis_index("scan") % 2 == 0
    leading, last = patterns[:1], patterns[count - 1 :]
    inner, outer = jnp.where(even, last, leading), jnp.where(even, leading, last)
    pairs = [(i, i + 1) for i in range(1, size - 1, 2)]
    inner = send(inner, 1)
    outer = lax.ppermute(outer, "scan", pairs + [(j, i) for i, j in pairs])
    rows, own, table, tail = arrange(patterns, templates, table)
    came, rows, own, table, tail, inner, outer = lax.optimization_barrier(
        (came, rows, own, table, tail, inner, outer)
    )
    part = lax.optimization_barrier(jnp.concatenate([own] + came, axis=0))
    parts, held = [part], [masks]
    for mask in middle:
        if mask != middle[0]:
            parts, held = [jnp.concatenate(parts, axis=0)], [held[0] + held[1]]
        parts, held = parts + [send(parts[0], mask)], held + [[m ^ mask for m in held[0]]]
    pat_spec = pattern_spectra(radius_bin, radial_gain, rows, tail, inner, outer, table)
    crossed = [[m ^ core for m in masks] for masks in held]
    early = [parts[0], send(parts[0], core)]
    total = orientation.shape[1]
    outs = jax.ShapeDtypeStruct((total, count), F32), jax.ShapeDtypeStruct((groups, count), F32)
    carry = match(pat_spec, table, inverse, early, [held[0], crossed[0]], [], total)
    last, pat_spec, carry = lax.optimization_barrier((parts[1], pat_spec, carry))
    over = send(last, core)
    carry = match(pat_spec, table, inverse, [last], [held[1]], carry, total)
    over, carry = lax.optimization_barrier((over, carry))
    corr, smooth = match(pat_spec, table, inverse, [over], [crossed[1]], carry, total, (orientation, *outs))
    return corr.T, smooth.T


def solution(mesh):
    placed = (P(("grp", "scan"), None, None), P("scan", None, None), P(), P(), P())
    return jax.shard_map(
        on_device,
        mesh=mesh,
        in_specs=placed,
        out_specs=(P(("grp", "scan"), None), P(("grp", "scan"), None)),
        check_vma=False,
    )
```
